128 devices in a mesh: tile: 8 (over z_lo, x), blk: 16 (over y, z_hi, core).
Axes of the slice: x: 4, y: 4, z: 4 (z_hi: 2, z_lo: 2; z = z_hi * 2 + z_lo), core: 2. Of those that a mesh axis runs over, the one named last changes fastest.
Arguments:
- tiles: bfloat16 [6144, 8, 8, 2048], P(('blk', 'tile')), may hold values from -10 to 10
- w_reduce: bfloat16 [2048, 512], replicated, may hold values from -0.125 to 0.125
- w_spatial: bfloat16 [9, 512, 512], replicated, may hold values from -0.09375 to 0.09375
- w_expand: bfloat16 [512, 2048], replicated, may hold values from -0.25 to 0.25
- w_embed: bfloat16 [2048, 1536], replicated, may hold values from -0.125 to 0.125
- w_query: bfloat16 [1536, 1536], P(None, 'tile'), may hold values from -8 to 8
- w_key: bfloat16 [1536, 1536], P(None, 'tile'), may hold values from -200 to 200
- w_value: bfloat16 [1536, 1536], P(None, 'tile'), may hold values from -0.15625 to 0.15625
- w_out: bfloat16 [1536, 1536], P('tile'), may hold values from -0.15625 to 0.15625
- slide_tiles: int32 [4], replicated, may hold values from 1 to 4608, 6144 in all
Outputs:
- mixed: bfloat16 [6144, 1536], P(('blk', 'tile'))
The draws below stay inside these ranges and needn't reach their ends.
Inputs may be any that keep to these rules, and one draw needn't show every extreme that they name: `slide_tiles`: the counts sum to 6144 and the largest is exactly 4608.
All inputs are finite; a program needn't handle non-finite values.
Results may differ from the reference program's by a relative error of at most 0.017.
Values may be sent and summed in bfloat16 or wider, within the bound.
A program may use at most 256 MiB of HBM per device.

```python
import math
import jax
import jax.numpy as jnp
import numpy as np
from jax import lax

C = 2048
MID = 512
SIDE = 8
E = 1536
HEADS = 16
HD = 96
SLIDES = 4
TOKENS = 6144
MOSTLEN = 4608


def draw_tiles(key, part):
    shape = (TOKENS, SIDE, SIDE, C)
    base = jax.random.normal(jax.random.fold_in(key, 1), shape, jnp.float32)
    offset = jax.random.normal(jax.random.fold_in(key, 2), (TOKENS, 1, 1, C), jnp.float32)
    return jnp.clip(base + offset, -10.0, 10.0).astype(jnp.bfloat16)


def query_key_pair(key):
    base = jax.random.normal(jax.random.fold_in(key, 11), (E, E), jnp.float32) / math.sqrt(E)
    other = jax.random.normal(jax.random.fold_in(key, 12), (E, E), jnp.float32) / math.sqrt(E)
    key_weight = other
    return (jnp.clip(base, -8.0, 8.0), jnp.clip(key_weight, -200.0, 200.0))


def draw_w_query(key, part):
    return query_key_pair(key)[0].astype(jnp.bfloat16)


def draw_w_key(key, part):
    return query_key_pair(key)[1].astype(jnp.bfloat16)


def block_levels(own_key, dims, shards, low, top_value):
    def one(axis_at, shards_of):
        heights = jax.random.uniform(jax.random.fold_in(jax.random.fold_in(own_key, 6), axis_at), (shards_of,), jnp.float32, low / len(shards), top_value / len(shards))
        return jnp.repeat(jnp.exp(heights), dims[axis_at] // shards_of).reshape((-1,) + (1,) * (len(dims) - axis_at - 1))

    factor_of = one(*shards[0])
    for cut in shards[1:]:
        factor_of = factor_of * one(*cut)
    return factor_of


def profile(number_of, total, bound, lean):
    portions = [(1 << 20) // math.isqrt(standing ** lean) + 1 for standing in range(2, number_of + 1)]
    rest, holding = total - bound - (number_of - 1), [1] * (number_of - 1)
    while rest > 0:
        candidates = [i for i in range(number_of - 1) if holding[i] < bound]
        mass, remaining = sum([portions[i] for i in candidates]), rest
        for i in candidates:
            extra = min(bound - holding[i], max(1, remaining * portions[i] // mass), rest)
            holding[i] = holding[i] + extra
            rest = rest - extra
    return np.array([bound] + holding)


def ragged_sizes(own_key, number_of, total, limit, lean):
    if number_of == 2:
        one = jax.random.randint(own_key, (), max(1, total - limit), min(limit, total - 1) + 1)
        return jnp.stack([one, total - one])
    sizes = jnp.asarray(profile(number_of, total, limit, lean), jnp.int32)
    twos = (number_of - 1) // 2
    source_of, sink = sizes[1:1 + 2 * twos:2], sizes[2:2 + 2 * twos:2]
    room = jnp.minimum(source_of - 1, limit - sink)
    passed = jax.random.randint(jax.random.fold_in(own_key, 1), (twos,), 0, 1 << 20) % (room + 1)
    sizes = sizes.at[1:1 + 2 * twos:2].set(source_of - passed).at[2:2 + 2 * twos:2].set(sink + passed)
    return sizes[jax.random.permutation(jax.random.fold_in(own_key, 2), number_of)]


def scatter_about(stream_key, dims, scale, reach, pieces=(), kind=jnp.bfloat16):
    array = scale * jax.random.normal(stream_key, dims, jnp.float32)
    if pieces:
        array = array * block_levels(stream_key, dims, pieces, -0.22, 0.18)
    return jnp.clip(array, -reach, reach).astype(kind)


def setup_inputs(seed: int = 0) -> dict:
    splits = jax.random.split(jax.random.key(seed), 11)
    return {
        "tiles": draw_tiles(jax.random.fold_in(splits[10], 71), 0),
        "w_reduce": scatter_about(splits[1], (C, MID), C ** -0.5, 0.125),
        "w_spatial": scatter_about(splits[2], (9, MID, MID), (9 * MID) ** -0.5, 0.09375),
        "w_expand": scatter_about(splits[3], (MID, C), MID ** -0.5, 0.25),
        "w_embed": scatter_about(splits[4], (C, E), C ** -0.5, 0.125),
        "w_query": draw_w_query(jax.random.fold_in(splits[10], 71), 0),
        "w_key": draw_w_key(jax.random.fold_in(splits[10], 71), 0),
        "w_value": scatter_about(splits[7], (E, E), E ** -0.5, 0.15625, ((1, 8),)),
        "w_out": scatter_about(splits[8], (E, E), E ** -0.5, 0.15625, ((0, 8),)),
        "slide_tiles": ragged_sizes(splits[9], SLIDES, TOKENS, MOSTLEN, 2).astype(jnp.int32),
    }


def encode(block, w_reduce, w_spatial, w_expand, w_embed):
    count = block.shape[0]
    flat = block.reshape(count * SIDE * SIDE, C)
    reduced = jax.nn.relu(jnp.dot(flat, w_reduce, preferred_element_type=jnp.float32)).astype(jnp.bfloat16)
    reduced = reduced.reshape(count, SIDE, SIDE, MID)
    padded = jnp.pad(reduced, ((0, 0), (1, 1), (1, 1), (0, 0)))
    summed = jnp.zeros((count * SIDE * SIDE, MID), jnp.float32)
    for tap in range(9):
        row_off = tap // 3
        col_off = tap % 3
        window = padded[:, row_off:row_off + SIDE, col_off:col_off + SIDE, :].reshape(count * SIDE * SIDE, MID)
        summed = summed + jnp.dot(window, w_spatial[tap], preferred_element_type=jnp.float32)
    spatial = jax.nn.relu(summed).astype(jnp.bfloat16)
    output = jax.nn.relu(flat.astype(jnp.float32) + jnp.dot(spatial, w_expand, preferred_element_type=jnp.float32))
    pooled = (lax.optimization_barrier(jnp.sum(output.reshape(count, SIDE * SIDE, C), axis=1)) / (SIDE * SIDE)).astype(jnp.bfloat16)
    return jnp.dot(pooled, w_embed, preferred_element_type=jnp.float32).astype(jnp.bfloat16)

def normalize(rows):
    values = rows.astype(jnp.float32)
    center = lax.optimization_barrier(jnp.mean(values, axis=1, keepdims=True))
    spread = lax.optimization_barrier(jnp.mean((values - center) ** 2, axis=1, keepdims=True))
    return ((values - center) * lax.rsqrt(spread + 1e-05)).astype(jnp.bfloat16)

def slide_of(positions, slide_tiles):
    ends = jnp.cumsum(slide_tiles)[:-1].astype(jnp.int32)
    return lax.optimization_barrier(jnp.sum((positions[:, None] >= ends[None, :]).astype(jnp.int32), axis=1))

def reference(tiles, w_reduce, w_spatial, w_expand, w_embed, w_query, w_key, w_value, w_out, slide_tiles):
    blocks = tiles.reshape(TOKENS // 16, 16, SIDE, SIDE, C)
    emb = lax.map(lambda block: encode(block, w_reduce, w_spatial, w_expand, w_embed), blocks).reshape(TOKENS, E)
    normed = normalize(emb)
    query = jnp.dot(normed, w_query, preferred_element_type=jnp.float32).astype(jnp.bfloat16)
    key = jnp.dot(normed, w_key, preferred_element_type=jnp.float32).astype(jnp.bfloat16)
    value = jnp.dot(normed, w_value, preferred_element_type=jnp.float32).astype(jnp.bfloat16)
    slide = slide_of(jnp.arange(TOKENS, dtype=jnp.int32), slide_tiles)
    same = slide[:, None] == slide[None, :]
    scale = 1.0 / math.sqrt(HD)

    def per_head(operands):
        head_query, head_key, head_value = operands
        scores = jnp.dot(head_query, head_key.T, preferred_element_type=jnp.float32) * scale
        scores = jnp.where(same, scores, -1e+30)
        top = lax.optimization_barrier(jnp.max(scores, axis=1, keepdims=True))
        probs = jnp.where(same, jnp.exp(scores - top), 0.0)
        total = lax.optimization_barrier(jnp.sum(probs, axis=1, keepdims=True))
        return jnp.dot(probs.astype(jnp.bfloat16), head_value, preferred_element_type=jnp.float32) / total
    split_query = query.reshape(TOKENS, HEADS, HD).transpose(1, 0, 2)
    split_key = key.reshape(TOKENS, HEADS, HD).transpose(1, 0, 2)
    split_value = value.reshape(TOKENS, HEADS, HD).transpose(1, 0, 2)
    heads_out = lax.map(per_head, (split_query, split_key, split_value))
    attended = heads_out.transpose(1, 0, 2).reshape(TOKENS, E).astype(jnp.bfloat16)
    mixed = emb.astype(jnp.float32) + jnp.dot(attended, w_out, preferred_element_type=jnp.float32)
    return mixed.astype(jnp.bfloat16)
```

```python
import math

import jax
import jax.numpy as jnp
from jax import lax
from jax.experimental import pallas as pl
from jax.experimental.pallas import tpu as pltpu
from jax.sharding import PartitionSpec as P

C = 2048
MID = 512
SIDE = 8
HD = 96


T = 16
R = T * 64
VMEM_LIMIT = 60 << 20


def encode_body(x_ref, wr_ref, ws_ref, wx_ref, we_ref, o_ref, p_ref, pool_ref):
    g = pl.program_id(0)

    @pl.when(g == 0)
    def _():
        p_ref[:, 0] = jnp.zeros((T, 8, 1536), jnp.bfloat16)
        p_ref[:, 9] = jnp.zeros((T, 8, 1536), jnp.bfloat16)

    x = x_ref[...].reshape(R, C)
    r = jnp.maximum(jnp.dot(x, wr_ref[...], preferred_element_type=jnp.float32), 0.0)
    j = lax.broadcasted_iota(jnp.int32, (R, MID), 0) % 8
    left = jnp.where(j == 0, 0.0, pltpu.roll(r, 1, 0))
    right = jnp.where(j == 7, 0.0, pltpu.roll(r, R - 1, 0))
    for at, shifted in enumerate((left, r, right)):
        p_ref[:, 1:9, :, at * MID : (at + 1) * MID] = shifted.astype(jnp.bfloat16).reshape(T, 8, 8, MID)
    acc = jnp.dot(p_ref[:, 0:8].reshape(R, 3 * MID), ws_ref[0], preferred_element_type=jnp.float32)
    acc += jnp.dot(p_ref[:, 1:9].reshape(R, 3 * MID), ws_ref[1], preferred_element_type=jnp.float32)
    acc += jnp.dot(p_ref[:, 2:10].reshape(R, 3 * MID), ws_ref[2], preferred_element_type=jnp.float32)
    s = jnp.maximum(acc, 0.0).astype(jnp.bfloat16)
    for c in range(4):
        cols = slice(c * 512, (c + 1) * 512)
        y = jnp.dot(s, wx_ref[:, cols], preferred_element_type=jnp.float32)
        y = jnp.maximum(y + x_ref[:, :, :, cols].reshape(R, 512).astype(jnp.float32), 0.0)
        y = jnp.sum(jnp.sum(y.reshape(T, 8, 8, 512), axis=1), axis=1) * (1.0 / 64)
        pool_ref[pl.ds(pl.multiple_of(g * T, T), T), cols] = y

    @pl.when(g == pl.num_programs(0) - 1)
    def _():
        o_ref[...] = jnp.dot(
            pool_ref[...].astype(jnp.bfloat16), we_ref[...], preferred_element_type=jnp.float32
        ).astype(jnp.bfloat16)


def encode(tiles, w_reduce, w_spatial, w_expand, w_embed):
    def full(s):
        return pl.BlockSpec(s, lambda g: (0,) * len(s), pipeline_mode=pl.Buffered(1))

    return pl.pallas_call(
        encode_body,
        grid=(48 // T,),
        in_specs=[
            pl.BlockSpec((T, 8, 8, C), lambda g: (g, 0, 0, 0)),
            full((C, MID)),
            full((3, 3 * MID, MID)),
            full((MID, C)),
            full((C, 1536)),
        ],
        out_specs=pl.BlockSpec((48, 1536), lambda g: (0, 0)),
        out_shape=jax.ShapeDtypeStruct((48, 1536), jnp.bfloat16),
        scratch_shapes=[
            pltpu.VMEM((T, 10, 8, 3 * MID), jnp.bfloat16),
            pltpu.VMEM((48, C), jnp.float32),
        ],
        compiler_params=pltpu.CompilerParams(vmem_limit_bytes=VMEM_LIMIT),
        name="encode",
    )(tiles, w_reduce, w_spatial.reshape(3, 3 * MID, MID), w_expand, w_embed)


def normalize(rows):
    values = rows.astype(jnp.float32)
    center = jnp.mean(values, axis=1, keepdims=True)
    spread = jnp.mean((values - center) ** 2, axis=1, keepdims=True)
    return ((values - center) * lax.rsqrt(spread + 1e-05)).astype(jnp.bfloat16)


def slide_of(positions, slide_tiles):
    ends = jnp.cumsum(slide_tiles)[:-1]
    return jnp.sum((positions[:, None] >= ends[None, :]).astype(jnp.int32), axis=1)


def shards(
    tiles, w_reduce, w_spatial, w_expand, w_embed, w_query, w_key, w_value, w_out, slide_tiles
):
    emb = encode(tiles, w_reduce, w_spatial, w_expand, w_embed)
    width = w_query.shape[1]
    heads_here = width // HD
    w_joined = jnp.concatenate([w_query, w_key, w_value], axis=1)
    joined = jnp.dot(
        normalize(lax.all_gather(emb, "tile", axis=0, tiled=True)),
        w_joined,
        preferred_element_type=jnp.float32,
    ).astype(jnp.bfloat16)
    length = joined.shape[0]
    query = joined[:, :width].reshape(length, heads_here, HD)
    key_value = joined[:, width:]
    query_pos = lax.axis_index("blk") * length + jnp.arange(length, dtype=jnp.int32)
    query_slide = slide_of(query_pos, slide_tiles)
    scale = 1.0 / math.sqrt(HD)
    piece = lax.all_gather(key_value, "blk", axis=0, tiled=True)
    rows = piece.shape[0]
    key_pos = jnp.arange(rows, dtype=jnp.int32)
    same = query_slide[:, None] == slide_of(key_pos, slide_tiles)[None, :]
    top_old = jnp.full((heads_here, length), -1e30, jnp.float32)
    keys = piece[:, :width].reshape(rows, heads_here, HD)
    values = piece[:, width:].reshape(rows, heads_here, HD)
    scores = jnp.einsum("qhd,khd->hqk", query, keys, preferred_element_type=jnp.float32) * scale
    scores = jnp.where(same[None], scores, -1e30)
    top_new = jnp.maximum(top_old, jnp.max(scores, axis=2))
    probs = jnp.where(same[None], jnp.exp(scores - top_new[:, :, None]), 0.0)
    total_new = jnp.sum(probs, axis=2)
    accum_new = jnp.einsum(
        "hqk,khd->hqd", probs.astype(jnp.bfloat16), values, preferred_element_type=jnp.float32
    )
    attended = (
        (accum_new / total_new[:, :, None])
        .transpose(1, 0, 2)
        .reshape(length, width)
        .astype(jnp.bfloat16)
    )
    summed = lax.psum_scatter(
        jnp.dot(attended, w_out, preferred_element_type=jnp.float32).astype(jnp.bfloat16),
        "tile",
        scatter_dimension=0,
        tiled=True,
    ).astype(jnp.float32)
    return (emb.astype(jnp.float32) + summed).astype(jnp.bfloat16)


def solution(mesh):
    placed = (
        P(("blk", "tile"), None, None, None),
        P(),
        P(),
        P(),
        P(),
        P(None, "tile"),
        P(None, "tile"),
        P(None, "tile"),
        P("tile", None),
        P(),
    )
    return jax.shard_map(
        shards, mesh=mesh, in_specs=placed, out_specs=P(("blk", "tile"), None), check_vma=False
    )
```

```python
import math

import jax
import jax.numpy as jnp
from jax import lax
from jax.experimental import pallas as pl
from jax.experimental.pallas import tpu as pltpu
from jax.sharding import PartitionSpec as P

C = 2048
MID = 512
SIDE = 8
HD = 96


T = 16
R = T * 64
VMEM_LIMIT = 60 << 20


def encode_body(x_ref, wr_ref, ws_ref, wx_ref, we_ref, o_ref, p_ref, pool_ref):
    g = pl.program_id(0)

    @pl.when(g == 0)
    def _():
        p_ref[:, 0] = jnp.zeros((T, 8, 1536), jnp.bfloat16)
        p_ref[:, 9] = jnp.zeros((T, 8, 1536), jnp.bfloat16)

    x = x_ref[...].reshape(R, C)
    r = jnp.maximum(jnp.dot(x, wr_ref[...], preferred_element_type=jnp.float32), 0.0)
    j = lax.broadcasted_iota(jnp.int32, (R, MID), 0) % 8
    left = jnp.where(j == 0, 0.0, pltpu.roll(r, 1, 0))
    right = jnp.where(j == 7, 0.0, pltpu.roll(r, R - 1, 0))
    for at, shifted in enumerate((left, r, right)):
        p_ref[:, 1:9, :, at * MID : (at + 1) * MID] = shifted.astype(jnp.bfloat16).reshape(T, 8, 8, MID)
    acc = jnp.dot(p_ref[:, 0:8].reshape(R, 3 * MID), ws_ref[0], preferred_element_type=jnp.float32)
    acc += jnp.dot(p_ref[:, 1:9].reshape(R, 3 * MID), ws_ref[1], preferred_element_type=jnp.float32)
    acc += jnp.dot(p_ref[:, 2:10].reshape(R, 3 * MID), ws_ref[2], preferred_element_type=jnp.float32)
    s = jnp.maximum(acc, 0.0).astype(jnp.bfloat16)
    for c in range(4):
        cols = slice(c * 512, (c + 1) * 512)
        y = jnp.dot(s, wx_ref[:, cols], preferred_element_type=jnp.float32)
        y = jnp.maximum(y + x_ref[:, :, :, cols].reshape(R, 512).astype(jnp.float32), 0.0)
        y = jnp.sum(jnp.sum(y.reshape(T, 8, 8, 512), axis=1), axis=1) * (1.0 / 64)
        pool_ref[pl.ds(pl.multiple_of(g * T, T), T), cols] = y

    @pl.when(g == pl.num_programs(0) - 1)
    def _():
        o_ref[...] = jnp.dot(
            pool_ref[...].astype(jnp.bfloat16), we_ref[...], preferred_element_type=jnp.float32
        ).astype(jnp.bfloat16)


def encode(tiles, w_reduce, w_spatial, w_expand, w_embed):
    def full(s):
        return pl.BlockSpec(s, lambda g: (0,) * len(s), pipeline_mode=pl.Buffered(1))

    return pl.pallas_call(
        encode_body,
        grid=(48 // T,),
        in_specs=[
            pl.BlockSpec((T, 8, 8, C), lambda g: (g, 0, 0, 0)),
            full((C, MID)),
            full((3, 3 * MID, MID)),
            full((MID, C)),
            full((C, 1536)),
        ],
        out_specs=pl.BlockSpec((48, 1536), lambda g: (0, 0)),
        out_shape=jax.ShapeDtypeStruct((48, 1536), jnp.bfloat16),
        scratch_shapes=[
            pltpu.VMEM((T, 10, 8, 3 * MID), jnp.bfloat16),
            pltpu.VMEM((48, C), jnp.float32),
        ],
        compiler_params=pltpu.CompilerParams(vmem_limit_bytes=VMEM_LIMIT),
        name="encode",
    )(tiles, w_reduce, w_spatial.reshape(3, 3 * MID, MID), w_expand, w_embed)


E = 1536
HEADS = 16
TILE_DEV = 8
BLK_DEV = 16
PER_DEV = 48
BLK_ROWS = PER_DEV * TILE_DEV
NEG = -1e30
MESH = pl.DeviceIdType.MESH


def normalize(rows):
    values = rows.astype(jnp.float32)
    center = jnp.mean(values, axis=1, keepdims=True)
    spread = jnp.mean((values - center) ** 2, axis=1, keepdims=True)
    return ((values - center) * lax.rsqrt(spread + 1e-05)).astype(jnp.bfloat16)


def nt(a, b):
    return lax.dot_general(a, b, (((1,), (1,)), ((), ())), preferred_element_type=jnp.float32)


def post_body(
    slides, emb_ref, wq_ref, wk_ref, wv_ref, wo_hbm, o_ref,
    wo_ref, emb_all, q_st, kv_st, q_all, kv_all, top, total, acc, att_st, att_in,
    local_sem, emb_send, emb_recv, kv_send, kv_recv, q_send, q_recv, att_send, att_recv,
):
    t = lax.axis_index("tile")
    b = lax.axis_index("blk")
    half = (b // 2) % 2
    partner = b + 2 - 4 * half

    def remote(src, dst, send, recv, tile, blk):
        return pltpu.make_async_remote_copy(
            src_ref=src, dst_ref=dst, send_sem=send, recv_sem=recv,
            device_id={"tile": tile, "blk": blk}, device_id_type=MESH,
        )

    load_out = pltpu.make_async_copy(wo_hbm, wo_ref, local_sem)
    load_out.start()
    barrier = pltpu.get_barrier_semaphore()
    for d in range(1, TILE_DEV):
        pl.semaphore_signal(barrier, inc=1, device_id={"tile": (t + d) % TILE_DEV, "blk": b}, device_id_type=MESH)
        pl.semaphore_signal(barrier, inc=1, device_id={"tile": (t + d) % TILE_DEV, "blk": partner}, device_id_type=MESH)
    for d in range(1, BLK_DEV):
        pl.semaphore_signal(barrier, inc=1, device_id={"tile": t, "blk": (b + d) % BLK_DEV}, device_id_type=MESH)
    pl.semaphore_wait(barrier, 2 * (TILE_DEV - 1) + BLK_DEV - 1)

    sends = [
        remote(emb_ref, emb_all.at[t], emb_send.at[d], emb_recv.at[t], (t + d) % TILE_DEV, b)
        for d in range(1, TILE_DEV)
    ]
    for copy in sends:
        copy.start()
    emb_all[t] = emb_ref[...]
    for d in range(1, TILE_DEV):
        src = (t + d) % TILE_DEV
        remote(emb_ref, emb_all.at[src], emb_send.at[d], emb_recv.at[src], src, b).wait_recv()
    normed = normalize(emb_all[...].reshape(BLK_ROWS, E))
    keys = nt(wk_ref[...], normed).astype(jnp.bfloat16)
    values = nt(wv_ref[...], normed).astype(jnp.bfloat16)
    for h in range(2):
        kv_st[h, 0:HD] = keys[h * HD : (h + 1) * HD]
        kv_st[h, HD : 2 * HD] = values[h * HD : (h + 1) * HD]
    for d in range(1, BLK_DEV):
        to = (b + d) % BLK_DEV
        copy = remote(kv_st.at[(to // 2) % 2], kv_all.at[b], kv_send.at[d], kv_recv.at[b], t, to)
        copy.start()
        sends.append(copy)
    queries = nt(wq_ref[...], normed).astype(jnp.bfloat16)
    for h in range(2):
        q_st[h] = queries[h * HD : (h + 1) * HD]
    q_copy = remote(q_st.at[1 - half], q_all, q_send, q_recv, t, partner)
    q_copy.start()
    sends.append(q_copy)
    kv_all[b] = kv_st[half]

    at = lax.broadcasted_iota(jnp.int32, (1, 2 * BLK_ROWS), 1)
    at = jnp.where(at < BLK_ROWS, b * BLK_ROWS + at, partner * BLK_ROWS + at - BLK_ROWS)
    low, high, end = jnp.zeros_like(at), jnp.zeros_like(at), 0
    for s in range(4):
        start, end = end, end + slides[s]
        inside = at >= start
        low = jnp.where(inside, start, low)
        high = jnp.where(inside, end, high)
    top[...] = jnp.full((1, 2 * BLK_ROWS), NEG, jnp.float32)
    total[...] = jnp.zeros((1, 2 * BLK_ROWS), jnp.float32)
    acc[...] = jnp.zeros((HD, 2 * BLK_ROWS), jnp.float32)
    q_copy.wait_recv()
    rate = 1.4426950408889634 / math.sqrt(HD)

    def visit(d, carry):
        src = (b + d) % BLK_DEV

        @pl.when(d > 0)
        def _():
            remote(kv_st.at[0], kv_all.at[src], kv_send.at[0], kv_recv.at[src], t, src).wait_recv()

        key = kv_all[src, 0:HD].T
        both = jnp.concatenate([q_st[half], q_all[...]], axis=1)
        scores = jnp.dot(key, both, preferred_element_type=jnp.float32) * rate
        pos = src * BLK_ROWS + lax.broadcasted_iota(jnp.int32, scores.shape, 0)
        scores = jnp.where((pos >= low) & (pos < high), scores, NEG)
        old = top[...]
        new = jnp.maximum(old, jnp.max(scores, axis=0, keepdims=True))
        weights = jnp.exp2(scores - new)
        keep = jnp.exp2(old - new)
        top[...] = new
        total[...] = total[...] * keep + jnp.sum(weights, axis=0, keepdims=True)
        acc[...] = acc[...] * keep + jnp.dot(
            kv_all[src, HD : 2 * HD], weights.astype(jnp.bfloat16), preferred_element_type=jnp.float32
        )
        return carry

    lax.fori_loop(0, BLK_DEV, visit, 0)

    att_st[:, HD:128] = jnp.zeros((2 * BLK_ROWS, 128 - HD), jnp.bfloat16)
    att_st[:, 0:HD] = (acc[...] / total[...]).T.astype(jnp.bfloat16)
    head = 2 * t + half
    for d in range(TILE_DEV):
        to = (t + d) % TILE_DEV
        for s, blk in enumerate((b, partner)):
            src = att_st.at[pl.ds(pl.multiple_of(s * BLK_ROWS + to * PER_DEV, PER_DEV), PER_DEV)]
            if d == 0 and s == 0:
                att_in[head] = att_st[pl.ds(pl.multiple_of(to * PER_DEV, PER_DEV), PER_DEV), :]
            else:
                copy = remote(src, att_in.at[head], att_send.at[2 * d + s], att_recv.at[head], to, blk)
                copy.start()
                sends.append(copy)
    for d in range(TILE_DEV):
        src = (t + d) % TILE_DEV
        for s, blk in enumerate((b, partner)):
            if d + s:
                from_head = 2 * src + (half if s == 0 else 1 - half)
                remote(
                    att_st.at[0:PER_DEV], att_in.at[from_head], att_send.at[0], att_recv.at[from_head], src, blk
                ).wait_recv()
    load_out.wait()
    attended = jnp.concatenate([att_in[h][:, 0:HD] for h in range(HEADS)], axis=1)
    mixed = jnp.dot(attended, wo_ref[...], preferred_element_type=jnp.float32)
    o_ref[...] = (emb_ref[...].astype(jnp.float32) + mixed).astype(jnp.bfloat16)
    for copy in sends:
        copy.wait_send()


def post(slide_tiles, emb, w_query, w_key, w_value, w_out):
    vmem = pl.BlockSpec(memory_space=pltpu.VMEM)
    bf = jnp.bfloat16
    dma = pltpu.SemaphoreType.DMA
    return pl.pallas_call(
        post_body,
        in_specs=[pl.BlockSpec(memory_space=pltpu.SMEM)] + [vmem] * 4 + [pl.BlockSpec(memory_space=pl.ANY)],
        out_specs=vmem,
        out_shape=jax.ShapeDtypeStruct((PER_DEV, E), bf),
        scratch_shapes=[
            pltpu.VMEM((E, E), bf),
            pltpu.VMEM((TILE_DEV, PER_DEV, E), bf),
            pltpu.VMEM((2, HD, BLK_ROWS), bf),
            pltpu.VMEM((2, 2 * HD, BLK_ROWS), bf),
            pltpu.VMEM((HD, BLK_ROWS), bf),
            pltpu.VMEM((BLK_DEV, 2 * HD, BLK_ROWS), bf),
            pltpu.VMEM((1, 2 * BLK_ROWS), jnp.float32),
            pltpu.VMEM((1, 2 * BLK_ROWS), jnp.float32),
            pltpu.VMEM((HD, 2 * BLK_ROWS), jnp.float32),
            pltpu.VMEM((2 * BLK_ROWS, 128), bf),
            pltpu.VMEM((HEADS, PER_DEV, 128), bf),
            dma, dma((8,)), dma((8,)), dma((16,)), dma((16,)), dma, dma, dma((16,)), dma((16,)),
        ],
        compiler_params=pltpu.CompilerParams(
            vmem_limit_bytes=VMEM_LIMIT, collective_id=0, has_side_effects=True
        ),
        name="post",
    )(slide_tiles, emb, w_query.T, w_key.T, w_value.T, w_out)


def shards(
    tiles, w_reduce, w_spatial, w_expand, w_embed, w_query, w_key, w_value, w_out, slide_tiles
):
    w_out_all = lax.all_gather(w_out, "tile", axis=0, tiled=True)
    emb = encode(tiles, w_reduce, w_spatial, w_expand, w_embed)
    return post(slide_tiles, emb, w_query, w_key, w_value, w_out_all)


def solution(mesh):
    placed = (
        P(("blk", "tile"), None, None, None),
        P(),
        P(),
        P(),
        P(),
        P(None, "tile"),
        P(None, "tile"),
        P(None, "tile"),
        P("tile", None),
        P(),
    )
    return jax.shard_map(
        shards, mesh=mesh, in_specs=placed, out_specs=P(("blk", "tile"), None), check_vma=False
    )
```

```python
import math

import jax
import jax.numpy as jnp
from jax import lax
from jax.experimental import pallas as pl
from jax.experimental.pallas import tpu as pltpu
from jax.sharding import PartitionSpec as P

C = 2048
MID = 512
HD = 96
E = 1536
HEADS = 16
TILE_DEV = 8
PER_DEV = 48
T = 16
CHUNKS = PER_DEV // T
R = T * 64
LANES = T * TILE_DEV
SHARD = PER_DEV * TILE_DEV
SLOTS = 16
QW = 2 * LANES
NEG = -1e30
RATE = 1.4426950408889634 / math.sqrt(HD)
VMEM_LIMIT = 61 << 20
MESH = pl.DeviceIdType.MESH
BF = jnp.bfloat16
F32 = jnp.float32


def normalize(rows):
    values = rows.astype(F32)
    center = jnp.mean(values, axis=1, keepdims=True)
    spread = jnp.mean((values - center) ** 2, axis=1, keepdims=True)
    return ((values - center) * lax.rsqrt(spread + 1e-05)).astype(BF)


def nt(a, b):
    return lax.dot_general(a, b, (((1,), (1,)), ((), ())), preferred_element_type=F32)


def body(
    slides, tiles, wr_hbm, ws_hbm, wx_hbm, we_hbm, wq_hbm, wk_hbm, wv_hbm, wo_hbm, o_ref,
    x_buf, wr, ws, wx, we, wq, wk, wv, wo, near, pool, emb, emb_all, q_st, kv_st, q_all, kv_all,
    key_slide, top, total, acc, att_st, att_in,
    x_sem, w_sem, own_sem, emb_send, emb_recv, kv_send, kv_recv, q_send, q_recv, att_send, att_recv,
    wo_send, wo_recv,
):
    t = lax.axis_index("tile")
    b = lax.axis_index("blk")
    core = b % 2
    half = (b // 2) % 2
    y = b // 4
    partner = b + 2 - 4 * half
    sibling = b + 1 - 2 * core
    x = t % 4
    z_lo = t // 4
    mine = 2 * y + half

    def remote(src, dst, send, recv, tile, blk):
        return pltpu.make_async_remote_copy(
            src_ref=src, dst_ref=dst, send_sem=send, recv_sem=recv,
            device_id={"tile": tile, "blk": blk}, device_id_type=MESH,
        )

    def load_x(c):
        return pltpu.make_async_copy(tiles.at[pl.ds(c * T, T)], x_buf.at[c % 2], x_sem.at[c % 2])

    weights = [
        pltpu.make_async_copy(a, v, w_sem.at[i])
        for i, (a, v) in enumerate(
            zip((wr_hbm, ws_hbm, wx_hbm, we_hbm, wk_hbm, wv_hbm, wq_hbm), (wr, ws, wx, we, wk, wv, wq))
        )
    ]
    load_x(0).start()
    for copy in weights:
        copy.start()

    def own_rows(p):
        return pltpu.make_async_copy(wo_hbm.at[pl.ds(p * HD, HD)], wo.at[2 * t + p], own_sem.at[p])

    def out_x(d):
        head = 2 * t + core
        rows = wo_hbm.at[pl.ds(core * HD, HD)]
        return remote(rows, wo.at[head], wo_send.at[d], wo_recv.at[head], z_lo * 4 + (x + d) % 4, b)

    def from_x(d):
        src = z_lo * 4 + (x + d) % 4
        head = 2 * src + core
        return remote(wo.at[head], wo.at[head], wo_send.at[0], wo_recv.at[head], src, b)

    z = 2 * half + z_lo

    def out_z(i):
        to = (z + (1 if i < 2 else 3)) % 4
        head = 2 * (z_lo * 4 + i) + core
        return remote(
            wo.at[head], wo.at[head], wo_send.at[4 + i], wo_recv.at[head],
            (to % 2) * 4 + x, y * 4 + (to // 2) * 2 + core,
        )

    def from_z(i):
        src = (z + (3 if i < 2 else 1)) % 4
        head = 2 * ((1 - z_lo) * 4 + i) + core
        return remote(
            wo.at[head], wo.at[head], wo_send.at[0], wo_recv.at[head],
            (src % 2) * 4 + x, y * 4 + (src // 2) * 2 + core,
        )

    def out_core(d):
        head = 2 * ((t + d) % TILE_DEV) + core
        return remote(wo.at[head], wo.at[head], wo_send.at[8 + d], wo_recv.at[head], t, sibling)

    def from_core(d):
        head = 2 * ((t + d) % TILE_DEV) + 1 - core
        return remote(wo.at[head], wo.at[head], wo_send.at[0], wo_recv.at[head], t, sibling)

    def out_emb(c, d):
        return remote(
            emb.at[c], emb_all.at[c, t], emb_send.at[c, d], emb_recv.at[c, t], (t + d) % TILE_DEV, b
        )

    def from_emb(c, d):
        src = (t + d) % TILE_DEV
        return remote(emb.at[c], emb_all.at[c, src], emb_send.at[c, d], emb_recv.at[c, src], src, b)

    def slot_of(c, s):
        return kv_all.at[c, :, pl.ds(pl.multiple_of(s * LANES, LANES), LANES)]

    def out_kv(c, i, same):
        to = ((y + i) % 4) * 4 + core + 2 * (half if same else 1 - half)
        return remote(
            kv_st.at[c, half if same else 1 - half], slot_of(c, mine),
            kv_send.at[c, 2 * i + (0 if same else 1)], kv_recv.at[c, mine], t, to,
        )

    def out_own(c):
        return remote(
            kv_st.at[c, half], slot_of(c, 8 + mine), kv_send.at[c, 0], kv_recv.at[c, 8 + mine], t, sibling
        )

    def from_kv(c, d):
        u = (mine + d) % 8
        return remote(
            kv_st.at[c, 0], slot_of(c, u), kv_send.at[c, 0], kv_recv.at[c, u], t, 2 * u + core
        )

    def pass_on(c, d):
        u = (mine + d) % 8
        return remote(
            slot_of(c, u), slot_of(c, 8 + u), kv_send.at[c, 8 + d], kv_recv.at[c, 8 + u], t, sibling
        )

    def from_sibling(c, u):
        return remote(
            kv_st.at[c, 0], slot_of(c, 8 + u), kv_send.at[c, 0], kv_recv.at[c, 8 + u], t, sibling
        )

    def swap_q(c):
        return remote(
            q_st.at[c], q_all.at[c, :, LANES:QW], q_send.at[c], q_recv.at[c], t, partner
        )

    barrier = pltpu.get_barrier_semaphore()
    for d in range(1, TILE_DEV):
        for blk in (b, partner):
            pl.semaphore_signal(
                barrier, inc=1, device_id={"tile": (t + d) % TILE_DEV, "blk": blk}, device_id_type=MESH
            )
    for d in range(1, 8):
        pl.semaphore_signal(
            barrier, inc=1, device_id={"tile": t, "blk": 2 * ((mine + d) % 8) + core}, device_id_type=MESH
        )
    pl.semaphore_signal(barrier, inc=1, device_id={"tile": t, "blk": sibling}, device_id_type=MESH)

    near[:, 0] = jnp.zeros((T, 8, 3 * MID), BF)
    near[:, 9] = jnp.zeros((T, 8, 3 * MID), BF)
    for h in range(2):
        own_rows(h).start()

    pl.semaphore_wait(barrier, 2 * (TILE_DEV - 1) + 8)
    for d in range(1, 4):
        out_x(d).start()

    ends = [slides[0], slides[0] + slides[1], slides[0] + slides[1] + slides[2]]

    def slide_at(pos):
        return sum((pos >= end).astype(jnp.int32) for end in ends)

    def table(i, carry):
        n = lax.broadcasted_iota(jnp.int32, (512, 128), 0) + 512 * (i % 4)
        slot = n >> 7
        blk = 2 * (slot & 7) + jnp.where(slot < 8, core, 1 - core)
        pos = blk * SHARD + ((n >> 4) & 7) * PER_DEV + (i // 4) * T + (n & 15)
        key_slide[pl.ds(pl.multiple_of(i * 512, 512), 512), :] = slide_at(pos)
        return carry

    n = lax.broadcasted_iota(jnp.int32, (8, CHUNKS * QW), 1)
    query_pos = (
        jnp.where(((n >> 7) & 1) == 0, b, partner) * SHARD + ((n >> 4) & 7) * PER_DEV + (n >> 8) * T + (n & 15)
    )
    query_slide = slide_at(query_pos)[0:1]
    top[...] = jnp.full((1, CHUNKS * QW), NEG, F32)
    total[...] = jnp.zeros((1, CHUNKS * QW), F32)
    acc[...] = jnp.zeros((HD, CHUNKS * QW), F32)

    def project(c):
        for d in range(1, TILE_DEV):
            from_emb(c, d).wait_recv()
        normed = normalize(emb_all[c].reshape(LANES, E))
        keys = nt(wk[...], normed).astype(BF)
        values = nt(wv[...], normed).astype(BF)
        for h in range(2):
            kv_st[c, h, 0:HD] = keys[h * HD : (h + 1) * HD]
            kv_st[c, h, HD : 2 * HD] = values[h * HD : (h + 1) * HD]
        for i in range(4):
            out_kv(c, i, False).start()
            if i:
                out_kv(c, i, True).start()
        out_own(c).start()
        kv_all[c, :, pl.ds(pl.multiple_of(mine * LANES, LANES), LANES)] = kv_st[c, half]
        queries = nt(wq[...], normed).astype(BF)
        first, second = queries[0:HD], queries[HD : 2 * HD]
        q_all[c, :, 0:LANES] = jnp.where(half == 0, first, second)
        q_st[c] = jnp.where(half == 0, second, first)
        swap_q(c).start()

    def relay(c):
        for d in range(1, 8):
            from_kv(c, d).wait_recv()
            pass_on(c, d).start()

    def attend(c, group, first, last):
        lanes = slice(first * QW, last * QW)
        at = pl.ds(pl.multiple_of(group * 512, 512), 512)
        key = kv_all[c, 0:HD, at].T
        query = jnp.concatenate([q_all[i] for i in range(first, last)], axis=1)
        scores = jnp.dot(key, query, preferred_element_type=F32) * RATE
        slide = key_slide[pl.ds(pl.multiple_of(c * 2048 + group * 512, 512), 512), :]
        slide = jnp.concatenate([slide] * ((last - first) * 2), axis=1)
        scores = jnp.where(slide == query_slide[:, lanes], scores, NEG)
        old = top[:, lanes]
        new = jnp.maximum(old, jnp.max(scores, axis=0, keepdims=True))
        weights = jnp.exp2(scores - new)
        keep = jnp.exp2(old - new)
        top[:, lanes] = new
        total[:, lanes] = total[:, lanes] * keep + jnp.sum(weights, axis=0, keepdims=True)
        acc[:, lanes] = acc[:, lanes] * keep + jnp.dot(
            kv_all[c, HD : 2 * HD, at], weights.astype(BF), preferred_element_type=F32
        )

    def encode(c, carry):
        load_x(c).wait()

        @pl.when(c < CHUNKS - 1)
        def _():
            load_x(c + 1).start()

        def first_use(i):
            @pl.when(c == 0)
            def _():
                weights[i].wait()

        first_use(0)
        x_ref = x_buf.at[c % 2]
        r = jnp.maximum(jnp.dot(x_ref[...].reshape(R, C), wr[...], preferred_element_type=F32), 0.0)
        j = lax.broadcasted_iota(jnp.int32, (R, MID), 0) % 8
        left = jnp.where(j == 0, 0.0, pltpu.roll(r, 1, 0))
        right = jnp.where(j == 7, 0.0, pltpu.roll(r, R - 1, 0))
        for at, shifted in enumerate((left, r, right)):
            near[:, 1:9, :, at * MID : (at + 1) * MID] = shifted.astype(BF).reshape(T, 8, 8, MID)
        first_use(1)
        conv = sum(
            jnp.dot(near[:, k : k + 8].reshape(R, 3 * MID), ws[k], preferred_element_type=F32) for k in range(3)
        )
        s = jnp.maximum(conv, 0.0).astype(BF)
        first_use(2)
        for k in range(4):
            cols = slice(k * 512, (k + 1) * 512)
            out = jnp.dot(s, wx[:, cols], preferred_element_type=F32)
            out = jnp.maximum(out + x_ref[:, :, :, cols].reshape(R, 512).astype(F32), 0.0)
            pool[:, cols] = (jnp.sum(jnp.sum(out.reshape(T, 8, 8, 512), axis=1), axis=1) * (1.0 / 64)).astype(BF)
        first_use(3)
        emb[c] = jnp.dot(pool[...], we[...], preferred_element_type=F32).astype(BF)
        for d in range(1, TILE_DEV):
            out_emb(c, d).start()
        emb_all[c, t] = emb[c]

        @pl.when(c == 0)
        def _():
            for i in range(4, 7):
                weights[i].wait()
            for h in range(2):
                own_rows(h).wait()
            for d in range(1, 4):
                from_x(d).wait_recv()
            for i in range(4):
                out_z(i).start()

        @pl.when(c > 0)
        def _():
            project(c - 1)

        @pl.when(c == 1)
        def _():
            for i in range(4):
                from_z(i).wait_recv()
            for d in range(1, TILE_DEV):
                out_core(d).start()

        return carry

    lax.fori_loop(0, CHUNKS, encode, 0)

    lax.fori_loop(0, 12, table, 0)
    relay(0)
    for c in range(2):
        swap_q(c).wait_recv()
    for u in range(8):
        from_sibling(0, u).wait_recv()
    lax.fori_loop(0, 4, lambda g, k: (attend(0, g, 0, 2), k)[1], 0)
    project(2)
    relay(1)
    swap_q(2).wait_recv()
    lax.fori_loop(0, 4, lambda g, k: (attend(0, g, 2, 3), k)[1], 0)
    for u in range(8):
        from_sibling(1, u).wait_recv()
    lax.fori_loop(0, 4, lambda g, k: (attend(1, g, 0, 3), k)[1], 0)
    relay(2)
    lax.fori_loop(0, 2, lambda g, k: (attend(2, g, 0, 3), k)[1], 0)
    for u in range(8):
        from_sibling(2, u).wait_recv()
    lax.fori_loop(2, 4, lambda g, k: (attend(2, g, 0, 3), k)[1], 0)

    result = (acc[...] / total[...]).T.astype(BF)
    att_st[...] = jnp.concatenate(
        [result, jnp.zeros((CHUNKS * QW, 128 - HD), BF)], axis=1
    ).reshape(CHUNKS, 2, TILE_DEV, T, 128)
    head = 2 * t + half

    def out_att(d, s):
        to = (t + d) % TILE_DEV
        return remote(
            att_st.at[:, s, to], att_in.at[head], att_send.at[2 * d + s], att_recv.at[head], to,
            partner if s else b,
        )

    def from_att(d, s):
        src = (t + d) % TILE_DEV
        other = 2 * src + (1 - half if s else half)
        return remote(
            att_st.at[:, s, 0], att_in.at[other], att_send.at[0], att_recv.at[other], src, partner if s else b
        )

    pairs = [(d, s) for d in range(TILE_DEV) for s in range(2) if d + s]
    for d, s in pairs:
        out_att(d, s).start()
    att_in[head] = att_st[:, 0, t]
    for d in range(1, TILE_DEV):
        from_core(d).wait_recv()
    for d, s in pairs:
        from_att(d, s).wait_recv()
    attended = jnp.concatenate([att_in[h].reshape(PER_DEV, 128)[:, 0:HD] for h in range(HEADS)], axis=1)
    mixed = jnp.dot(attended, wo[...].reshape(E, E), preferred_element_type=F32)
    o_ref[...] = (emb[...].reshape(PER_DEV, E).astype(F32) + mixed).astype(BF)

    for d, s in pairs:
        out_att(d, s).wait_send()
    for d in range(1, 4):
        out_x(d).wait_send()
    for i in range(4):
        out_z(i).wait_send()
    for d in range(1, TILE_DEV):
        out_core(d).wait_send()
    for c in range(CHUNKS):
        for d in range(1, TILE_DEV):
            out_emb(c, d).wait_send()
        for i in range(4):
            out_kv(c, i, False).wait_send()
            if i:
                out_kv(c, i, True).wait_send()
        out_own(c).wait_send()
        for d in range(1, 8):
            pass_on(c, d).wait_send()
        swap_q(c).wait_send()


def shards(
    tiles, w_reduce, w_spatial, w_expand, w_embed, w_query, w_key, w_value, w_out, slide_tiles
):
    anywhere = pl.BlockSpec(memory_space=pl.ANY)
    dma = pltpu.SemaphoreType.DMA
    vmem = pltpu.VMEM
    width = 2 * HD
    return pl.pallas_call(
        body,
        in_specs=[pl.BlockSpec(memory_space=pltpu.SMEM)] + [anywhere] * 9,
        out_specs=pl.BlockSpec(memory_space=vmem),
        out_shape=jax.ShapeDtypeStruct((PER_DEV, E), BF),
        scratch_shapes=[
            vmem((2, T, 8, 8, C), BF),
            vmem((C, MID), BF),
            vmem((3, 3 * MID, MID), BF),
            vmem((MID, C), BF),
            vmem((C, E), BF),
            vmem((width, E), BF),
            vmem((width, E), BF),
            vmem((width, E), BF),
            vmem((HEADS, HD, E), BF),
            vmem((T, 10, 8, 3 * MID), BF),
            vmem((T, C), BF),
            vmem((CHUNKS, T, E), BF),
            vmem((CHUNKS, TILE_DEV, T, E), BF),
            vmem((CHUNKS, HD, LANES), BF),
            vmem((CHUNKS, 2, width, LANES), BF),
            vmem((CHUNKS, HD, QW), BF),
            vmem((CHUNKS, width, SLOTS * LANES), BF),
            vmem((CHUNKS * SLOTS * LANES, 128), jnp.int32),
            vmem((1, CHUNKS * QW), F32),
            vmem((1, CHUNKS * QW), F32),
            vmem((HD, CHUNKS * QW), F32),
            vmem((CHUNKS, 2, TILE_DEV, T, 128), BF),
            vmem((HEADS, CHUNKS, T, 128), BF),
            dma((2,)), dma((7,)), dma((2,)),
            dma((CHUNKS, 8)), dma((CHUNKS, 8)),
            dma((CHUNKS, 16)), dma((CHUNKS, 16)),
            dma((CHUNKS,)), dma((CHUNKS,)),
            dma((16,)), dma((16,)),
            dma((16,)), dma((16,)),
        ],
        compiler_params=pltpu.CompilerParams(
            vmem_limit_bytes=VMEM_LIMIT, collective_id=0, has_side_effects=True
        ),
        name="slide_step",
    )(
        slide_tiles, tiles, w_reduce, w_spatial.reshape(3, 3 * MID, MID), w_expand, w_embed,
        w_query.T, w_key.T, w_value.T, w_out,
    )


def solution(mesh):
    placed = (
        P(("blk", "tile"), None, None, None),
        P(),
        P(),
        P(),
        P(),
        P(None, "tile"),
        P(None, "tile"),
        P(None, "tile"),
        P("tile", None),
        P(),
    )
    return jax.shard_map(
        shards, mesh=mesh, in_specs=placed, out_specs=P(("blk", "tile"), None), check_vma=False
    )
```

```python
import math

import jax
import jax.numpy as jnp
from jax import lax
from jax.experimental import pallas as pl
from jax.experimental.pallas import tpu as pltpu
from jax.sharding import PartitionSpec as P

C = 2048
MID = 512
HD = 96
E = 1536
HEADS = 16
TILE_DEV = 8
PER_DEV = 48
T = 16
CHUNKS = PER_DEV // T
R = T * 64
LANES = T * TILE_DEV
SHARD = PER_DEV * TILE_DEV
SLOTS = 16
QW = 2 * LANES
NEG = -1e30
RATE = 1.4426950408889634 / math.sqrt(HD)
VMEM_LIMIT = 61 << 20
MESH = pl.DeviceIdType.MESH
BF = jnp.bfloat16
F32 = jnp.float32


def normalize(rows):
    values = rows.astype(F32)
    center = jnp.mean(values, axis=1, keepdims=True)
    spread = jnp.mean((values - center) ** 2, axis=1, keepdims=True)
    return ((values - center) * lax.rsqrt(spread + 1e-05)).astype(BF)


def nt(a, b):
    return lax.dot_general(a, b, (((1,), (1,)), ((), ())), preferred_element_type=F32)


def body(
    slides, tiles, wr_hbm, ws_hbm, wx_hbm, we_hbm, wq_hbm, wk_hbm, wv_hbm, wo_hbm, o_ref,
    x_buf, wr, ws, wx, we, wqkv, wo, near, pool, emb, emb_all, q_st, kv_st, q_all, kv_all,
    key_slide, top, total, acc, att_st, att_in,
    x_sem, w_sem, own_sem, emb_send, emb_recv, kv_send, kv_recv, q_send, q_recv, att_send, att_recv,
    wo_send, wo_recv,
):
    t = lax.axis_index("tile")
    b = lax.axis_index("blk")
    core = b % 2
    half = (b // 2) % 2
    y = b // 4
    partner = b + 2 - 4 * half
    sibling = b + 1 - 2 * core
    x = t % 4
    z_lo = t // 4
    mine = 2 * y + half

    def remote(src, dst, send, recv, tile, blk):
        return pltpu.make_async_remote_copy(
            src_ref=src, dst_ref=dst, send_sem=send, recv_sem=recv,
            device_id={"tile": tile, "blk": blk}, device_id_type=MESH,
        )

    def load_x(c):
        return pltpu.make_async_copy(tiles.at[pl.ds(c * T, T)], x_buf.at[c % 2], x_sem.at[c % 2])

    weights = [
        pltpu.make_async_copy(a, v, w_sem.at[i])
        for i, (a, v) in enumerate(
            zip((wr_hbm, ws_hbm, wx_hbm, we_hbm, wk_hbm, wv_hbm, wq_hbm), (wr, ws, wx, we, wqkv.at[0], wqkv.at[1], wqkv.at[2]))
        )
    ]
    load_x(0).start()
    for copy in weights:
        copy.start()

    def own_rows(p):
        return pltpu.make_async_copy(wo_hbm.at[pl.ds(p * HD, HD)], wo.at[2 * t + p], own_sem.at[p])

    def out_x(d):
        head = 2 * t + core
        rows = wo_hbm.at[pl.ds(core * HD, HD)]
        return remote(rows, wo.at[head], wo_send.at[d], wo_recv.at[head], z_lo * 4 + (x + d) % 4, b)

    def from_x(d):
        src = z_lo * 4 + (x + d) % 4
        head = 2 * src + core
        return remote(wo.at[head], wo.at[head], wo_send.at[0], wo_recv.at[head], src, b)

    z = 2 * half + z_lo

    def out_z(i):
        to = (z + (1 if i < 2 else 3)) % 4
        head = 2 * (z_lo * 4 + i) + core
        return remote(
            wo.at[head], wo.at[head], wo_send.at[4 + i], wo_recv.at[head],
            (to % 2) * 4 + x, y * 4 + (to // 2) * 2 + core,
        )

    def from_z(i):
        src = (z + (3 if i < 2 else 1)) % 4
        head = 2 * ((1 - z_lo) * 4 + i) + core
        return remote(
            wo.at[head], wo.at[head], wo_send.at[0], wo_recv.at[head],
            (src % 2) * 4 + x, y * 4 + (src // 2) * 2 + core,
        )

    def out_core(d):
        head = 2 * ((t + d) % TILE_DEV) + core
        return remote(wo.at[head], wo.at[head], wo_send.at[8 + d], wo_recv.at[head], t, sibling)

    def from_core(d):
        head = 2 * ((t + d) % TILE_DEV) + 1 - core
        return remote(wo.at[head], wo.at[head], wo_send.at[0], wo_recv.at[head], t, sibling)

    def out_emb(c, d):
        return remote(
            emb.at[c], emb_all.at[c, t], emb_send.at[c, d], emb_recv.at[c, t], (t + d) % TILE_DEV, b
        )

    def from_emb(c, d):
        src = (t + d) % TILE_DEV
        return remote(emb.at[c], emb_all.at[c, src], emb_send.at[c, d], emb_recv.at[c, src], src, b)

    def slot_of(c, s):
        return kv_all.at[c, :, pl.ds(pl.multiple_of(s * LANES, LANES), LANES)]

    def out_kv(c, i, same):
        to = ((y + i) % 4) * 4 + core + 2 * (half if same else 1 - half)
        return remote(
            kv_st.at[c, half if same else 1 - half], slot_of(c, mine),
            kv_send.at[c, 2 * i + (0 if same else 1)], kv_recv.at[c, mine], t, to,
        )

    def out_own(c):
        return remote(
            kv_st.at[c, half], slot_of(c, 8 + mine), kv_send.at[c, 0], kv_recv.at[c, 8 + mine], t, sibling
        )

    def from_kv(c, d):
        u = (mine + d) % 8
        return remote(
            kv_st.at[c, 0], slot_of(c, u), kv_send.at[c, 0], kv_recv.at[c, u], t, 2 * u + core
        )

    def pass_on(c, d):
        u = (mine + d) % 8
        return remote(
            slot_of(c, u), slot_of(c, 8 + u), kv_send.at[c, 8 + d], kv_recv.at[c, 8 + u], t, sibling
        )

    def from_sibling(c, u):
        return remote(
            kv_st.at[c, 0], slot_of(c, 8 + u), kv_send.at[c, 0], kv_recv.at[c, 8 + u], t, sibling
        )

    def swap_q(c):
        return remote(
            q_st.at[c], q_all.at[c, :, LANES:QW], q_send.at[c], q_recv.at[c], t, partner
        )

    barrier = pltpu.get_barrier_semaphore()
    for d in range(1, TILE_DEV):
        for blk in (b, partner):
            pl.semaphore_signal(
                barrier, inc=1, device_id={"tile": (t + d) % TILE_DEV, "blk": blk}, device_id_type=MESH
            )
    for d in range(1, 8):
        pl.semaphore_signal(
            barrier, inc=1, device_id={"tile": t, "blk": 2 * ((mine + d) % 8) + core}, device_id_type=MESH
        )
    pl.semaphore_signal(barrier, inc=1, device_id={"tile": t, "blk": sibling}, device_id_type=MESH)

    near[:, 0] = jnp.zeros((T, 8, 3 * MID), BF)
    near[:, 9] = jnp.zeros((T, 8, 3 * MID), BF)
    for h in range(2):
        own_rows(h).start()

    pl.semaphore_wait(barrier, 2 * (TILE_DEV - 1) + 8)
    for d in range(1, 4):
        out_x(d).start()

    ends = [slides[0], slides[0] + slides[1], slides[0] + slides[1] + slides[2]]

    def slide_at(pos):
        return sum((pos >= end).astype(jnp.int32) for end in ends)

    def table(i, carry):
        n = lax.broadcasted_iota(jnp.int32, (512, 128), 0) + 512 * (i % 4)
        slot = n >> 7
        blk = 2 * (slot & 7) + jnp.where(slot < 8, core, 1 - core)
        pos = blk * SHARD + ((n >> 4) & 7) * PER_DEV + (i // 4) * T + (n & 15)
        key_slide[pl.ds(pl.multiple_of(i * 512, 512), 512), :] = slide_at(pos)
        return carry

    n = lax.broadcasted_iota(jnp.int32, (8, CHUNKS * QW), 1)
    query_pos = (
        jnp.where(((n >> 7) & 1) == 0, b, partner) * SHARD + ((n >> 4) & 7) * PER_DEV + (n >> 8) * T + (n & 15)
    )
    query_slide = slide_at(query_pos)[0:1]
    top[...] = jnp.full((1, CHUNKS * QW), NEG, F32)
    total[...] = jnp.zeros((1, CHUNKS * QW), F32)
    acc[...] = jnp.zeros((HD, CHUNKS * QW), F32)

    def project(c):
        for d in range(1, TILE_DEV):
            from_emb(c, d).wait_recv()
        normed = normalize(emb_all[c].reshape(LANES, E))
        joined = nt(wqkv[...].reshape(6 * HD, E), normed).astype(BF)
        for h in range(2):
            kv_st[c, h, 0:HD] = joined[h * HD : (h + 1) * HD]
            kv_st[c, h, HD : 2 * HD] = joined[(2 + h) * HD : (3 + h) * HD]
        for i in range(4):
            out_kv(c, i, False).start()
            if i:
                out_kv(c, i, True).start()
        out_own(c).start()
        kv_all[c, :, pl.ds(pl.multiple_of(mine * LANES, LANES), LANES)] = kv_st[c, half]
        first, second = joined[4 * HD : 5 * HD], joined[5 * HD : 6 * HD]
        q_all[c, :, 0:LANES] = jnp.where(half == 0, first, second)
        q_st[c] = jnp.where(half == 0, second, first)
        swap_q(c).start()

    def relay(c):
        for d in range(1, 8):
            from_kv(c, d).wait_recv()
            pass_on(c, d).start()

    def attend(c, group, first, last):
        lanes = slice(first * QW, last * QW)
        at = pl.ds(pl.multiple_of(group * 512, 512), 512)
        key = kv_all[c, 0:HD, at].T
        query = jnp.concatenate([q_all[i] for i in range(first, last)], axis=1)
        scores = jnp.dot(key, query, preferred_element_type=F32) * RATE
        slide = key_slide[pl.ds(pl.multiple_of(c * 2048 + group * 512, 512), 512), :]
        slide = jnp.concatenate([slide] * ((last - first) * 2), axis=1)
        scores = jnp.where(slide == query_slide[:, lanes], scores, NEG)
        old = top[:, lanes]
        new = jnp.maximum(old, jnp.max(scores, axis=0, keepdims=True))
        weights = jnp.exp2(scores - new)
        keep = jnp.exp2(old - new)
        top[:, lanes] = new
        total[:, lanes] = total[:, lanes] * keep + jnp.sum(weights, axis=0, keepdims=True)
        acc[:, lanes] = acc[:, lanes] * keep + jnp.dot(
            kv_all[c, HD : 2 * HD, at], weights.astype(BF), preferred_element_type=F32
        )

    def encode(c, carry):
        load_x(c).wait()

        @pl.when(c < CHUNKS - 1)
        def _():
            load_x(c + 1).start()

        def first_use(i):
            @pl.when(c == 0)
            def _():
                weights[i].wait()

        first_use(0)
        x_ref = x_buf.at[c % 2]
        r = jnp.maximum(jnp.dot(x_ref[...].reshape(R, C), wr[...], preferred_element_type=F32), 0.0)
        j = lax.broadcasted_iota(jnp.int32, (R, MID), 0) % 8
        left = jnp.where(j == 0, 0.0, pltpu.roll(r, 1, 0))
        right = jnp.where(j == 7, 0.0, pltpu.roll(r, R - 1, 0))
        for at, shifted in enumerate((left, r, right)):
            near[:, 1:9, :, at * MID : (at + 1) * MID] = shifted.astype(BF).reshape(T, 8, 8, MID)
        first_use(1)
        conv = sum(
            jnp.dot(near[:, k : k + 8].reshape(R, 3 * MID), ws[k], preferred_element_type=F32) for k in range(3)
        )
        s = jnp.maximum(conv, 0.0).astype(BF)
        first_use(2)

        @pl.when(c == 1)
        def _():
            for d in range(1, 4):
                from_x(d).wait_recv()
            for i in range(4):
                out_z(i).start()

        for k in range(4):
            cols = slice(k * 512, (k + 1) * 512)
            out = jnp.dot(s, wx[:, cols], preferred_element_type=F32)
            out = jnp.maximum(out + x_ref[:, :, :, cols].reshape(R, 512).astype(F32), 0.0)
            pool[:, cols] = (jnp.sum(jnp.sum(out.reshape(T, 8, 8, 512), axis=1), axis=1) * (1.0 / 64)).astype(BF)
        first_use(3)
        emb[c] = jnp.dot(pool[...], we[...], preferred_element_type=F32).astype(BF)
        for d in range(1, TILE_DEV):
            out_emb(c, d).start()
        emb_all[c, t] = emb[c]

        @pl.when(c == 0)
        def _():
            for i in range(4, 7):
                weights[i].wait()
            for h in range(2):
                own_rows(h).wait()

        @pl.when(c == CHUNKS - 1)
        def _():
            relay(0)

        @pl.when(c > 0)
        def _():
            project(c - 1)

        return carry

    lax.fori_loop(0, CHUNKS, encode, 0)

    lax.fori_loop(0, 12, table, 0)
    for i in range(4):
        from_z(i).wait_recv()
    for d in range(1, TILE_DEV):
        out_core(d).start()
    for c in range(2):
        swap_q(c).wait_recv()
    for u in range(8):
        from_sibling(0, u).wait_recv()
    lax.fori_loop(0, 4, lambda g, k: (attend(0, g, 0, 2), k)[1], 0)
    project(2)
    relay(1)
    swap_q(2).wait_recv()
    lax.fori_loop(0, 4, lambda g, k: (attend(0, g, 2, 3), k)[1], 0)
    for u in range(8):
        from_sibling(1, u).wait_recv()
    lax.fori_loop(0, 4, lambda g, k: (attend(1, g, 0, 3), k)[1], 0)
    relay(2)
    lax.fori_loop(0, 2, lambda g, k: (attend(2, g, 0, 3), k)[1], 0)
    for u in range(8):
        from_sibling(2, u).wait_recv()
    lax.fori_loop(2, 4, lambda g, k: (attend(2, g, 0, 3), k)[1], 0)

    result = (acc[...] / total[...]).T.astype(BF)
    att_st[...] = jnp.concatenate(
        [result, jnp.zeros((CHUNKS * QW, 128 - HD), BF)], axis=1
    ).reshape(CHUNKS, 2, TILE_DEV, T, 128)
    head = 2 * t + half

    def out_att(d, s):
        to = (t + d) % TILE_DEV
        return remote(
            att_st.at[:, s, to], att_in.at[head], att_send.at[2 * d + s], att_recv.at[head], to,
            partner if s else b,
        )

    def from_att(d, s):
        src = (t + d) % TILE_DEV
        other = 2 * src + (1 - half if s else half)
        return remote(
            att_st.at[:, s, 0], att_in.at[other], att_send.at[0], att_recv.at[other], src, partner if s else b
        )

    pairs = [(d, s) for d in range(TILE_DEV) for s in range(2) if d + s]
    for d, s in pairs:
        out_att(d, s).start()
    att_in[head] = att_st[:, 0, t]
    for d in range(1, TILE_DEV):
        from_core(d).wait_recv()
    for d, s in pairs:
        from_att(d, s).wait_recv()
    attended = jnp.concatenate([att_in[h].reshape(PER_DEV, 128)[:, 0:HD] for h in range(HEADS)], axis=1)
    mixed = jnp.dot(attended, wo[...].reshape(E, E), preferred_element_type=F32)
    o_ref[...] = (emb[...].reshape(PER_DEV, E).astype(F32) + mixed).astype(BF)

    for d, s in pairs:
        out_att(d, s).wait_send()
    for d in range(1, 4):
        out_x(d).wait_send()
    for i in range(4):
        out_z(i).wait_send()
    for d in range(1, TILE_DEV):
        out_core(d).wait_send()
    for c in range(CHUNKS):
        for d in range(1, TILE_DEV):
            out_emb(c, d).wait_send()
        for i in range(4):
            out_kv(c, i, False).wait_send()
            if i:
                out_kv(c, i, True).wait_send()
        out_own(c).wait_send()
        for d in range(1, 8):
            pass_on(c, d).wait_send()
        swap_q(c).wait_send()


def shards(
    tiles, w_reduce, w_spatial, w_expand, w_embed, w_query, w_key, w_value, w_out, slide_tiles
):
    anywhere = pl.BlockSpec(memory_space=pl.ANY)
    dma = pltpu.SemaphoreType.DMA
    vmem = pltpu.VMEM
    width = 2 * HD
    return pl.pallas_call(
        body,
        in_specs=[pl.BlockSpec(memory_space=pltpu.SMEM)] + [anywhere] * 9,
        out_specs=pl.BlockSpec(memory_space=vmem),
        out_shape=jax.ShapeDtypeStruct((PER_DEV, E), BF),
        scratch_shapes=[
            vmem((2, T, 8, 8, C), BF),
            vmem((C, MID), BF),
            vmem((3, 3 * MID, MID), BF),
            vmem((MID, C), BF),
            vmem((C, E), BF),
            vmem((3, width, E), BF),
            vmem((HEADS, HD, E), BF),
            vmem((T, 10, 8, 3 * MID), BF),
            vmem((T, C), BF),
            vmem((CHUNKS, T, E), BF),
            vmem((CHUNKS, TILE_DEV, T, E), BF),
            vmem((CHUNKS, HD, LANES), BF),
            vmem((CHUNKS, 2, width, LANES), BF),
            vmem((CHUNKS, HD, QW), BF),
            vmem((CHUNKS, width, SLOTS * LANES), BF),
            vmem((CHUNKS * SLOTS * LANES, 128), jnp.int32),
            vmem((1, CHUNKS * QW), F32),
            vmem((1, CHUNKS * QW), F32),
            vmem((HD, CHUNKS * QW), F32),
            vmem((CHUNKS, 2, TILE_DEV, T, 128), BF),
            vmem((HEADS, CHUNKS, T, 128), BF),
            dma((2,)), dma((7,)), dma((2,)),
            dma((CHUNKS, 8)), dma((CHUNKS, 8)),
            dma((CHUNKS, 16)), dma((CHUNKS, 16)),
            dma((CHUNKS,)), dma((CHUNKS,)),
            dma((16,)), dma((16,)),
            dma((16,)), dma((16,)),
        ],
        compiler_params=pltpu.CompilerParams(
            vmem_limit_bytes=VMEM_LIMIT, collective_id=0, has_side_effects=True
        ),
        name="slide_step",
    )(
        slide_tiles, tiles, w_reduce, w_spatial.reshape(3, 3 * MID, MID), w_expand, w_embed,
        w_query.T, w_key.T, w_value.T, w_out,
    )


def solution(mesh):
    placed = (
        P(("blk", "tile"), None, None, None),
        P(),
        P(),
        P(),
        P(),
        P(None, "tile"),
        P(None, "tile"),
        P(None, "tile"),
        P("tile", None),
        P(),
    )
    return jax.shard_map(
        shards, mesh=mesh, in_specs=placed, out_specs=P(("blk", "tile"), None), check_vma=False
    )
```

```python
import math

import jax
import jax.numpy as jnp
from jax import lax
from jax.experimental import pallas as pl
from jax.experimental.pallas import tpu as pltpu
from jax.sharding import PartitionSpec as P

C = 2048
MID = 512
HD = 96
E = 1536
HEADS = 16
TILE_DEV = 8
PER_DEV = 48
T = 16
CHUNKS = PER_DEV // T
R = T * 64
LANES = T * TILE_DEV
SHARD = PER_DEV * TILE_DEV
SLOTS = 16
QW = 2 * LANES
NEG = -1e30
RATE = 1.4426950408889634 / math.sqrt(HD)
VMEM_LIMIT = 61 << 20
MESH = pl.DeviceIdType.MESH
BF = jnp.bfloat16
F32 = jnp.float32


def normalize(rows):
    values = rows.astype(F32)
    center = jnp.mean(values, axis=1, keepdims=True)
    spread = jnp.mean((values - center) ** 2, axis=1, keepdims=True)
    return ((values - center) * lax.rsqrt(spread + 1e-05)).astype(BF)


def nt(a, b):
    return lax.dot_general(a, b, (((1,), (1,)), ((), ())), preferred_element_type=F32)


def body(
    slides, tiles, wr_hbm, ws_hbm, wx_hbm, we_hbm, wq_hbm, wk_hbm, wv_hbm, wo_hbm, o_ref,
    x_buf, wr, ws, wx, we, wqkv, wo, near, pool, emb, emb_all, q_st, kv_st, q_all, kv_all,
    key_slide, top, total, acc, att_st, att_in,
    x_sem, w_sem, own_sem, emb_send, emb_recv, kv_send, kv_recv, q_send, q_recv, att_send, att_recv,
    wo_send, wo_recv,
):
    t = lax.axis_index("tile")
    b = lax.axis_index("blk")
    core = b % 2
    half = (b // 2) % 2
    y = b // 4
    partner = b + 2 - 4 * half
    sibling = b + 1 - 2 * core
    x = t % 4
    z_lo = t // 4
    mine = 2 * y + half

    def remote(src, dst, send, recv, tile, blk):
        return pltpu.make_async_remote_copy(
            src_ref=src, dst_ref=dst, send_sem=send, recv_sem=recv,
            device_id={"tile": tile, "blk": blk}, device_id_type=MESH,
        )

    def load_x(c):
        return pltpu.make_async_copy(tiles.at[pl.ds(c * T, T)], x_buf.at[c % 2], x_sem.at[c % 2])

    weights = [
        pltpu.make_async_copy(a, v, w_sem.at[i])
        for i, (a, v) in enumerate(
            zip((wr_hbm, ws_hbm, wx_hbm, we_hbm, wk_hbm, wv_hbm, wq_hbm), (wr, ws, wx, we, wqkv.at[0], wqkv.at[1], wqkv.at[2]))
        )
    ]
    load_x(0).start()
    for copy in weights:
        copy.start()

    own_rows = pltpu.make_async_copy(wo_hbm.at[pl.ds(core * HD, HD)], wo.at[core, t], own_sem)

    def out_x(d):
        rows = wo_hbm.at[pl.ds(core * HD, HD)]
        return remote(rows, wo.at[core, t], wo_send.at[d], wo_recv.at[x], z_lo * 4 + (x + d) % 4, b)

    def from_x(d):
        src = (x + d) % 4
        there = wo.at[core, z_lo * 4 + src]
        return remote(there, there, wo_send.at[0], wo_recv.at[src], z_lo * 4 + src, b)

    z = 2 * half + z_lo

    def out_z(i):
        to = (z + (3 if i else 1)) % 4
        rows = wo.at[core, pl.ds(z_lo * 4 + 2 * i, 2)]
        return remote(
            rows, rows, wo_send.at[4 + i], wo_recv.at[4 + i],
            (to % 2) * 4 + x, y * 4 + (to // 2) * 2 + core,
        )

    def from_z(i):
        src = (z + (1 if i else 3)) % 4
        rows = wo.at[core, pl.ds((1 - z_lo) * 4 + 2 * i, 2)]
        return remote(
            rows, rows, wo_send.at[0], wo_recv.at[4 + i],
            (src % 2) * 4 + x, y * 4 + (src // 2) * 2 + core,
        )

    def out_core():
        return remote(wo.at[core], wo.at[core], wo_send.at[6], wo_recv.at[6], t, sibling)

    def from_core():
        return remote(wo.at[1 - core], wo.at[1 - core], wo_send.at[6], wo_recv.at[6], t, sibling)

    def out_emb(c, d):
        return remote(
            emb.at[c], emb_all.at[c, t], emb_send.at[c, d], emb_recv.at[c, t], (t + d) % TILE_DEV, b
        )

    def from_emb(c, d):
        src = (t + d) % TILE_DEV
        return remote(emb.at[c], emb_all.at[c, src], emb_send.at[c, d], emb_recv.at[c, src], src, b)

    def slot_of(c, s):
        return kv_all.at[c, :, pl.ds(pl.multiple_of(s * LANES, LANES), LANES)]

    def out_kv(c, i, same):
        to = ((y + i) % 4) * 4 + core + 2 * (half if same else 1 - half)
        return remote(
            kv_st.at[c, half if same else 1 - half], slot_of(c, mine),
            kv_send.at[c, 2 * i + (0 if same else 1)], kv_recv.at[c, mine], t, to,
        )

    def from_kv(c, d):
        u = (mine + d) % 8
        return remote(
            kv_st.at[c, 0], slot_of(c, u), kv_send.at[c, 0], kv_recv.at[c, u], t, 2 * u + core
        )

    def pass_on(c):
        row = SLOTS // 2 * LANES
        return remote(
            kv_all.at[c, :, 0:row], kv_all.at[c, :, row : 2 * row], kv_send.at[c, 8], kv_recv.at[c, 8], t, sibling
        )

    def swap_q(c):
        return remote(
            q_st.at[c], q_all.at[c, :, LANES:QW], q_send.at[c], q_recv.at[c], t, partner
        )

    barrier = pltpu.get_barrier_semaphore()
    for d in range(1, TILE_DEV):
        for blk in (b, partner):
            pl.semaphore_signal(
                barrier, inc=1, device_id={"tile": (t + d) % TILE_DEV, "blk": blk}, device_id_type=MESH
            )
    for d in range(1, 8):
        pl.semaphore_signal(
            barrier, inc=1, device_id={"tile": t, "blk": 2 * ((mine + d) % 8) + core}, device_id_type=MESH
        )
    pl.semaphore_signal(barrier, inc=1, device_id={"tile": t, "blk": sibling}, device_id_type=MESH)

    near[:, 0] = jnp.zeros((T, 8, 3 * MID), BF)
    near[:, 9] = jnp.zeros((T, 8, 3 * MID), BF)
    own_rows.start()

    pl.semaphore_wait(barrier, 2 * (TILE_DEV - 1) + 8)
    for d in range(1, 4):
        out_x(d).start()

    ends = [slides[0], slides[0] + slides[1], slides[0] + slides[1] + slides[2]]

    def slide_at(pos):
        return sum((pos >= end).astype(jnp.int32) for end in ends)

    def table(i, carry):
        n = lax.broadcasted_iota(jnp.int32, (512, 128), 0) + 512 * (i % 4)
        slot = n >> 7
        blk = 2 * (slot & 7) + jnp.where(slot < 8, core, 1 - core)
        pos = blk * SHARD + ((n >> 4) & 7) * PER_DEV + (i // 4) * T + (n & 15)
        key_slide[pl.ds(pl.multiple_of(i * 512, 512), 512), :] = slide_at(pos)
        return carry

    n = lax.broadcasted_iota(jnp.int32, (8, CHUNKS * QW), 1)
    query_pos = (
        jnp.where(((n >> 7) & 1) == 0, b, partner) * SHARD + ((n >> 4) & 7) * PER_DEV + (n >> 8) * T + (n & 15)
    )
    query_slide = slide_at(query_pos)[0:1]
    top[...] = jnp.full((1, CHUNKS * QW), NEG, F32)
    total[...] = jnp.zeros((1, CHUNKS * QW), F32)
    acc[...] = jnp.zeros((HD, CHUNKS * QW), F32)

    def project(c):
        for d in range(1, TILE_DEV):
            from_emb(c, d).wait_recv()
        normed = normalize(emb_all[c].reshape(LANES, E))
        joined = nt(wqkv[...].reshape(6 * HD, E), normed).astype(BF)
        for h in range(2):
            kv_st[c, h, 0:HD] = joined[h * HD : (h + 1) * HD]
            kv_st[c, h, HD : 2 * HD] = joined[(2 + h) * HD : (3 + h) * HD]
        for i in range(4):
            out_kv(c, i, False).start()
            if i:
                out_kv(c, i, True).start()
        kv_all[c, :, pl.ds(pl.multiple_of(mine * LANES, LANES), LANES)] = kv_st[c, half]
        first, second = joined[4 * HD : 5 * HD], joined[5 * HD : 6 * HD]
        q_all[c, :, 0:LANES] = jnp.where(half == 0, first, second)
        q_st[c] = jnp.where(half == 0, second, first)
        swap_q(c).start()

    def relay(c):
        for d in range(1, 8):
            from_kv(c, d).wait_recv()
        pass_on(c).start()

    def attend(c, group, first, last):
        lanes = slice(first * QW, last * QW)
        at = pl.ds(pl.multiple_of(group * 512, 512), 512)
        key = kv_all[c, 0:HD, at].T
        query = jnp.concatenate([q_all[i] for i in range(first, last)], axis=1)
        scores = jnp.dot(key, query, preferred_element_type=F32) * RATE
        slide = key_slide[pl.ds(pl.multiple_of(c * 2048 + group * 512, 512), 512), :]
        slide = jnp.concatenate([slide] * ((last - first) * 2), axis=1)
        scores = jnp.where(slide == query_slide[:, lanes], scores, NEG)
        old = top[:, lanes]
        new = jnp.maximum(old, jnp.max(scores, axis=0, keepdims=True))
        weights = jnp.exp2(scores - new)
        keep = jnp.exp2(old - new)
        top[:, lanes] = new
        total[:, lanes] = total[:, lanes] * keep + jnp.sum(weights, axis=0, keepdims=True)
        acc[:, lanes] = acc[:, lanes] * keep + jnp.dot(
            kv_all[c, HD : 2 * HD, at], weights.astype(BF), preferred_element_type=F32
        )

    def encode(c, carry):
        load_x(c).wait()

        @pl.when(c < CHUNKS - 1)
        def _():
            load_x(c + 1).start()

        def first_use(i):
            @pl.when(c == 0)
            def _():
                weights[i].wait()

        first_use(0)
        x_ref = x_buf.at[c % 2]
        r = jnp.maximum(jnp.dot(x_ref[...].reshape(R, C), wr[...], preferred_element_type=F32), 0.0)
        j = lax.broadcasted_iota(jnp.int32, (R, MID), 0) % 8
        left = jnp.where(j == 0, 0.0, pltpu.roll(r, 1, 0))
        right = jnp.where(j == 7, 0.0, pltpu.roll(r, R - 1, 0))
        for at, shifted in enumerate((left, r, right)):
            near[:, 1:9, :, at * MID : (at + 1) * MID] = shifted.astype(BF).reshape(T, 8, 8, MID)
        first_use(1)
        conv = sum(
            jnp.dot(near[:, k : k + 8].reshape(R, 3 * MID), ws[k], preferred_element_type=F32) for k in range(3)
        )
        s = jnp.maximum(conv, 0.0).astype(BF)
        first_use(2)

        @pl.when(c == 1)
        def _():
            for d in range(1, 4):
                from_x(d).wait_recv()
            for i in range(2):
                out_z(i).start()

        for k in range(4):
            cols = slice(k * 512, (k + 1) * 512)
            out = jnp.dot(s, wx[:, cols], preferred_element_type=F32)
            out = jnp.maximum(out + x_ref[:, :, :, cols].reshape(R, 512).astype(F32), 0.0)
            pool[:, cols] = (jnp.sum(jnp.sum(out.reshape(T, 8, 8, 512), axis=1), axis=1) * (1.0 / 64)).astype(BF)
        first_use(3)
        emb[c] = jnp.dot(pool[...], we[...], preferred_element_type=F32).astype(BF)
        for d in range(1, TILE_DEV):
            out_emb(c, d).start()
        emb_all[c, t] = emb[c]

        @pl.when(c == 0)
        def _():
            for i in range(4, 7):
                weights[i].wait()
            own_rows.wait()

        @pl.when(c == CHUNKS - 1)
        def _():
            relay(0)

        @pl.when(c > 0)
        def _():
            project(c - 1)

        return carry

    lax.fori_loop(0, CHUNKS, encode, 0)

    lax.fori_loop(0, 12, table, 0)
    for c in range(2):
        swap_q(c).wait_recv()
    pass_on(0).wait_recv()
    lax.fori_loop(0, 4, lambda g, k: (attend(0, g, 0, 2), k)[1], 0)
    project(2)
    relay(1)
    swap_q(2).wait_recv()
    lax.fori_loop(0, 4, lambda g, k: (attend(0, g, 2, 3), k)[1], 0)
    pass_on(1).wait_recv()
    lax.fori_loop(0, 4, lambda g, k: (attend(1, g, 0, 3), k)[1], 0)
    relay(2)
    for i in range(2):
        from_z(i).wait_recv()
    out_core().start()
    lax.fori_loop(0, 2, lambda g, k: (attend(2, g, 0, 3), k)[1], 0)
    pass_on(2).wait_recv()
    lax.fori_loop(2, 4, lambda g, k: (attend(2, g, 0, 3), k)[1], 0)

    result = (acc[...] / total[...]).T.astype(BF)
    att_st[...] = jnp.concatenate(
        [result, jnp.zeros((CHUNKS * QW, 128 - HD), BF)], axis=1
    ).reshape(CHUNKS, 2, TILE_DEV, T, 128)
    head = 2 * t + half

    def out_att(d, s):
        to = (t + d) % TILE_DEV
        return remote(
            att_st.at[:, s, to], att_in.at[head], att_send.at[2 * d + s], att_recv.at[head], to,
            partner if s else b,
        )

    def from_att(d, s):
        src = (t + d) % TILE_DEV
        other = 2 * src + (1 - half if s else half)
        return remote(
            att_st.at[:, s, 0], att_in.at[other], att_send.at[0], att_recv.at[other], src, partner if s else b
        )

    pairs = [(d, s) for d in range(TILE_DEV) for s in range(2) if d + s]
    for d, s in pairs:
        out_att(d, s).start()
    att_in[head] = att_st[:, 0, t]
    for d in range(1, 4):
        out_x(d).wait_send()
    for i in range(2):
        out_z(i).wait_send()
    for c in range(CHUNKS):
        for d in range(1, TILE_DEV):
            out_emb(c, d).wait_send()
        for i in range(4):
            out_kv(c, i, False).wait_send()
            if i:
                out_kv(c, i, True).wait_send()
        pass_on(c).wait_send()
        swap_q(c).wait_send()
    out_core().wait_send()
    from_core().wait_recv()
    for d, s in pairs:
        from_att(d, s).wait_recv()
    attended = jnp.concatenate([att_in[2 * k + p].reshape(PER_DEV, 128)[:, 0:HD] for p in range(2) for k in range(TILE_DEV)], axis=1)
    mixed = jnp.dot(attended, wo[...].reshape(E, E), preferred_element_type=F32)
    o_ref[...] = (emb[...].reshape(PER_DEV, E).astype(F32) + mixed).astype(BF)

    for d, s in pairs:
        out_att(d, s).wait_send()


def shards(
    tiles, w_reduce, w_spatial, w_expand, w_embed, w_query, w_key, w_value, w_out, slide_tiles
):
    anywhere = pl.BlockSpec(memory_space=pl.ANY)
    dma = pltpu.SemaphoreType.DMA
    vmem = pltpu.VMEM
    width = 2 * HD
    return pl.pallas_call(
        body,
        in_specs=[pl.BlockSpec(memory_space=pltpu.SMEM)] + [anywhere] * 9,
        out_specs=pl.BlockSpec(memory_space=vmem),
        out_shape=jax.ShapeDtypeStruct((PER_DEV, E), BF),
        scratch_shapes=[
            vmem((2, T, 8, 8, C), BF),
            vmem((C, MID), BF),
            vmem((3, 3 * MID, MID), BF),
            vmem((MID, C), BF),
            vmem((C, E), BF),
            vmem((3, width, E), BF),
            vmem((2, TILE_DEV, HD, E), BF),
            vmem((T, 10, 8, 3 * MID), BF),
            vmem((T, C), BF),
            vmem((CHUNKS, T, E), BF),
            vmem((CHUNKS, TILE_DEV, T, E), BF),
            vmem((CHUNKS, HD, LANES), BF),
            vmem((CHUNKS, 2, width, LANES), BF),
            vmem((CHUNKS, HD, QW), BF),
            vmem((CHUNKS, width, SLOTS * LANES), BF),
            vmem((CHUNKS * SLOTS * LANES, 128), jnp.int32),
            vmem((1, CHUNKS * QW), F32),
            vmem((1, CHUNKS * QW), F32),
            vmem((HD, CHUNKS * QW), F32),
            vmem((CHUNKS, 2, TILE_DEV, T, 128), BF),
            vmem((HEADS, CHUNKS, T, 128), BF),
            dma((2,)), dma((7,)), dma,
            dma((CHUNKS, 8)), dma((CHUNKS, 8)),
            dma((CHUNKS, 16)), dma((CHUNKS, 16)),
            dma((CHUNKS,)), dma((CHUNKS,)),
            dma((16,)), dma((16,)),
            dma((16,)), dma((16,)),
        ],
        compiler_params=pltpu.CompilerParams(
            vmem_limit_bytes=VMEM_LIMIT, collective_id=0, has_side_effects=True
        ),
        name="slide_step",
    )(
        slide_tiles, tiles, w_reduce, w_spatial.reshape(3, 3 * MID, MID), w_expand, w_embed,
        w_query.T, w_key.T, w_value.T, w_out,
    )


def solution(mesh):
    placed = (
        P(("blk", "tile"), None, None, None),
        P(),
        P(),
        P(),
        P(),
        P(None, "tile"),
        P(None, "tile"),
        P(None, "tile"),
        P("tile", None),
        P(),
    )
    return jax.shard_map(
        shards, mesh=mesh, in_specs=placed, out_specs=P(("blk", "tile"), None), check_vma=False
    )
```

```python
import math

import jax
import jax.numpy as jnp
from jax import lax
from jax.experimental import pallas as pl
from jax.experimental.pallas import tpu as pltpu
from jax.sharding import PartitionSpec as P

C = 2048
MID = 512
HD = 96
E = 1536
HEADS = 16
TILE_DEV = 8
PER_DEV = 48
T = 16
CHUNKS = PER_DEV // T
R = T * 64
LANES = T * TILE_DEV
SHARD = PER_DEV * TILE_DEV
SLOTS = 16
QW = 2 * LANES
NEG = -1e30
RATE = 1.4426950408889634 / math.sqrt(HD)
VMEM_LIMIT = 61 << 20
MESH = pl.DeviceIdType.MESH
BF = jnp.bfloat16
F32 = jnp.float32


def normalize(rows):
    values = rows.astype(F32)
    center = jnp.mean(values, axis=1, keepdims=True)
    spread = jnp.mean((values - center) ** 2, axis=1, keepdims=True)
    return ((values - center) * lax.rsqrt(spread + 1e-05)).astype(BF)


def nt(a, b):
    return lax.dot_general(a, b, (((1,), (1,)), ((), ())), preferred_element_type=F32)


def body(
    slides, tiles, wr_hbm, ws_hbm, wx_hbm, we_hbm, wq_hbm, wk_hbm, wv_hbm, wo_hbm, o_ref,
    x_buf, wr, ws, wx, we, wqkv, wo, near, pool, emb, emb_all, q_st, kv_st, q_all, kv_all,
    key_slide, top, total, acc, att_st, att_in,
    x_sem, w_sem, own_sem, emb_send, emb_recv, kv_send, kv_recv, q_send, q_recv, att_send, att_recv,
    wo_send, wo_recv,
):
    t = lax.axis_index("tile")
    b = lax.axis_index("blk")
    core = b % 2
    half = (b // 2) % 2
    y = b // 4
    partner = b + 2 - 4 * half
    sibling = b + 1 - 2 * core
    x = t % 4
    z_lo = t // 4
    mine = 2 * y + half

    def remote(src, dst, send, recv, tile, blk):
        return pltpu.make_async_remote_copy(
            src_ref=src, dst_ref=dst, send_sem=send, recv_sem=recv,
            device_id={"tile": tile, "blk": blk}, device_id_type=MESH,
        )

    def load_x(c):
        return pltpu.make_async_copy(tiles.at[pl.ds(c * T, T)], x_buf.at[c % 2], x_sem.at[c % 2])

    weights = [
        pltpu.make_async_copy(a, v, w_sem.at[i])
        for i, (a, v) in enumerate(
            zip((wr_hbm, ws_hbm, wx_hbm, we_hbm, wk_hbm, wv_hbm, wq_hbm), (wr, ws, wx, we, wqkv.at[0], wqkv.at[1], wqkv.at[2]))
        )
    ]
    load_x(0).start()
    for copy in weights:
        copy.start()

    own_rows = pltpu.make_async_copy(wo_hbm.at[pl.ds(core * HD, HD)], wo.at[core, t], own_sem)

    def out_x(d):
        rows = wo_hbm.at[pl.ds(core * HD, HD)]
        return remote(rows, wo.at[core, t], wo_send.at[d], wo_recv.at[x], z_lo * 4 + (x + d) % 4, b)

    def from_x(d):
        src = (x + d) % 4
        there = wo.at[core, z_lo * 4 + src]
        return remote(there, there, wo_send.at[0], wo_recv.at[src], z_lo * 4 + src, b)

    z = 2 * half + z_lo

    def out_z(i):
        to = (z + (3 if i else 1)) % 4
        rows = wo.at[core, pl.ds(z_lo * 4 + 2 * i, 2)]
        return remote(
            rows, rows, wo_send.at[4 + i], wo_recv.at[4 + i],
            (to % 2) * 4 + x, y * 4 + (to // 2) * 2 + core,
        )

    def from_z(i):
        src = (z + (1 if i else 3)) % 4
        rows = wo.at[core, pl.ds((1 - z_lo) * 4 + 2 * i, 2)]
        return remote(
            rows, rows, wo_send.at[0], wo_recv.at[4 + i],
            (src % 2) * 4 + x, y * 4 + (src // 2) * 2 + core,
        )

    def out_core():
        return remote(wo.at[core], wo.at[core], wo_send.at[6], wo_recv.at[6], t, sibling)

    def from_core():
        return remote(wo.at[1 - core], wo.at[1 - core], wo_send.at[6], wo_recv.at[6], t, sibling)

    def out_emb(c, d):
        return remote(
            emb.at[c], emb_all.at[c, t], emb_send.at[c, d], emb_recv.at[c, t], (t + d) % TILE_DEV, b
        )

    def from_emb(c, d):
        src = (t + d) % TILE_DEV
        return remote(emb.at[c], emb_all.at[c, src], emb_send.at[c, d], emb_recv.at[c, src], src, b)

    def slot_of(c, s):
        return kv_all.at[c, :, pl.ds(pl.multiple_of(s * LANES, LANES), LANES)]

    def out_kv(c, i, same):
        to = ((y + i) % 4) * 4 + core + 2 * (half if same else 1 - half)
        return remote(
            kv_st.at[c, half if same else 1 - half], slot_of(c, mine),
            kv_send.at[c, 2 * i + (0 if same else 1)], kv_recv.at[c, mine], t, to,
        )

    def from_kv(c, d):
        u = (mine + d) % 8
        return remote(
            kv_st.at[c, 0], slot_of(c, u), kv_send.at[c, 0], kv_recv.at[c, u], t, 2 * u + core
        )

    def pass_on(c):
        row = SLOTS // 2 * LANES
        return remote(
            kv_all.at[c, :, 0:row], kv_all.at[c, :, row : 2 * row], kv_send.at[c, 8], kv_recv.at[c, 8], t, sibling
        )

    def swap_q(c):
        return remote(
            q_st.at[c], q_all.at[c, :, LANES:QW], q_send.at[c], q_recv.at[c], t, partner
        )

    barrier = pltpu.get_barrier_semaphore()
    for d in range(1, TILE_DEV):
        for blk in (b, partner):
            pl.semaphore_signal(
                barrier, inc=1, device_id={"tile": (t + d) % TILE_DEV, "blk": blk}, device_id_type=MESH
            )
    for d in range(1, 8):
        pl.semaphore_signal(
            barrier, inc=1, device_id={"tile": t, "blk": 2 * ((mine + d) % 8) + core}, device_id_type=MESH
        )
    pl.semaphore_signal(barrier, inc=1, device_id={"tile": t, "blk": sibling}, device_id_type=MESH)

    near[:, 0] = jnp.zeros((T, 8, 3 * MID), BF)
    near[:, 9] = jnp.zeros((T, 8, 3 * MID), BF)
    own_rows.start()

    pl.semaphore_wait(barrier, 2 * (TILE_DEV - 1) + 8)
    for d in range(1, 4):
        out_x(d).start()

    ends = [slides[0], slides[0] + slides[1], slides[0] + slides[1] + slides[2]]

    def slide_at(pos):
        return sum((pos >= end).astype(jnp.int32) for end in ends)

    def table(i, carry):
        n = lax.broadcasted_iota(jnp.int32, (512, 128), 0) + 512 * (i % 4)
        slot = n >> 7
        blk = 2 * (slot & 7) + jnp.where(slot < 8, core, 1 - core)
        pos = blk * SHARD + ((n >> 4) & 7) * PER_DEV + (i // 4) * T + (n & 15)
        key_slide[pl.ds(pl.multiple_of(i * 512, 512), 512), :] = slide_at(pos)
        return carry

    n = lax.broadcasted_iota(jnp.int32, (8, CHUNKS * QW), 1)
    query_pos = (
        jnp.where(((n >> 7) & 1) == 0, b, partner) * SHARD + ((n >> 4) & 7) * PER_DEV + (n >> 8) * T + (n & 15)
    )
    query_slide = slide_at(query_pos)[0:1]
    top[...] = jnp.full((1, CHUNKS * QW), NEG, F32)
    total[...] = jnp.zeros((1, CHUNKS * QW), F32)
    acc[...] = jnp.zeros((HD, CHUNKS * QW), F32)

    lax.fori_loop(0, 12, table, 0)

    def project(c):
        for d in range(1, TILE_DEV):
            from_emb(c, d).wait_recv()
        normed = normalize(emb_all[c].reshape(LANES, E))
        joined = nt(wqkv[...].reshape(6 * HD, E), normed).astype(BF)
        for h in range(2):
            kv_st[c, h, 0:HD] = joined[h * HD : (h + 1) * HD]
            kv_st[c, h, HD : 2 * HD] = joined[(2 + h) * HD : (3 + h) * HD]
        for i in range(4):
            out_kv(c, i, False).start()
            if i:
                out_kv(c, i, True).start()
        kv_all[c, :, pl.ds(pl.multiple_of(mine * LANES, LANES), LANES)] = kv_st[c, half]
        first, second = joined[4 * HD : 5 * HD], joined[5 * HD : 6 * HD]
        q_all[c, :, 0:LANES] = jnp.where(half == 0, first, second)
        q_st[c] = jnp.where(half == 0, second, first)
        swap_q(c).start()

    def relay(c):
        for d in range(1, 8):
            from_kv(c, d).wait_recv()
        pass_on(c).start()

    def attend(c, group, first, last):
        lanes = slice(first * QW, last * QW)
        at = pl.ds(pl.multiple_of(group * 512, 512), 512)
        key = kv_all[c, 0:HD, at].T
        query = jnp.concatenate([q_all[i] for i in range(first, last)], axis=1)
        scores = jnp.dot(key, query, preferred_element_type=F32) * RATE
        slide = key_slide[pl.ds(pl.multiple_of(c * 2048 + group * 512, 512), 512), :]
        slide = jnp.concatenate([slide] * ((last - first) * 2), axis=1)
        scores = jnp.where(slide == query_slide[:, lanes], scores, NEG)
        old = top[:, lanes]
        new = jnp.maximum(old, jnp.max(scores, axis=0, keepdims=True))
        weights = jnp.exp2(scores - new)
        keep = jnp.exp2(old - new)
        top[:, lanes] = new
        total[:, lanes] = total[:, lanes] * keep + jnp.sum(weights, axis=0, keepdims=True)
        acc[:, lanes] = acc[:, lanes] * keep + jnp.dot(
            kv_all[c, HD : 2 * HD, at], weights.astype(BF), preferred_element_type=F32
        )

    def encode(c, carry):
        load_x(c).wait()

        @pl.when(c < CHUNKS - 1)
        def _():
            load_x(c + 1).start()

        def first_use(i):
            @pl.when(c == 0)
            def _():
                weights[i].wait()

        first_use(0)
        x_ref = x_buf.at[c % 2]
        r = jnp.maximum(jnp.dot(x_ref[...].reshape(R, C), wr[...], preferred_element_type=F32), 0.0)
        j = lax.broadcasted_iota(jnp.int32, (R, MID), 0) % 8
        left = jnp.where(j == 0, 0.0, pltpu.roll(r, 1, 0))
        right = jnp.where(j == 7, 0.0, pltpu.roll(r, R - 1, 0))
        for at, shifted in enumerate((left, r, right)):
            near[:, 1:9, :, at * MID : (at + 1) * MID] = shifted.astype(BF).reshape(T, 8, 8, MID)
        first_use(1)
        conv = sum(
            jnp.dot(near[:, k : k + 8].reshape(R, 3 * MID), ws[k], preferred_element_type=F32) for k in range(3)
        )
        s = jnp.maximum(conv, 0.0).astype(BF)
        first_use(2)

        @pl.when(c > 0)
        def _():
            project(c - 1)

        @pl.when(c == 1)
        def _():
            for d in range(1, 4):
                from_x(d).wait_recv()
            for i in range(2):
                out_z(i).start()

        for k in range(4):
            cols = slice(k * 512, (k + 1) * 512)
            out = jnp.dot(s, wx[:, cols], preferred_element_type=F32)
            out = jnp.maximum(out + x_ref[:, :, :, cols].reshape(R, 512).astype(F32), 0.0)
            pool[:, cols] = (jnp.sum(jnp.sum(out.reshape(T, 8, 8, 512), axis=1), axis=1) * (1.0 / 64)).astype(BF)
        first_use(3)
        emb[c] = jnp.dot(pool[...], we[...], preferred_element_type=F32).astype(BF)
        for d in range(1, TILE_DEV):
            out_emb(c, d).start()
        emb_all[c, t] = emb[c]

        @pl.when(c == 0)
        def _():
            for i in range(4, 7):
                weights[i].wait()
            own_rows.wait()

        @pl.when(c > 0)
        def _():
            relay(c - 1)

        return carry

    lax.fori_loop(0, CHUNKS, encode, 0)

    def sweep(c, first, last, start=0, stop=4):
        def block(g, carry):
            attend(c, g, first, last)
            return carry

        lax.fori_loop(start, stop, block, 0)

    for c in range(2):
        swap_q(c).wait_recv()
    for c in range(2):
        pass_on(c).wait_recv()
        sweep(c, 0, 2)
    project(2)
    swap_q(2).wait_recv()
    sweep(0, 2, 3)
    relay(2)
    sweep(1, 2, 3)
    for i in range(2):
        from_z(i).wait_recv()
    out_core().start()
    sweep(2, 0, 3, 0, 2)
    pass_on(2).wait_recv()
    sweep(2, 0, 3, 2, 4)

    result = (acc[...] / total[...]).T.astype(BF)
    att_st[...] = jnp.concatenate(
        [result, jnp.zeros((CHUNKS * QW, 128 - HD), BF)], axis=1
    ).reshape(CHUNKS, 2, TILE_DEV, T, 128)
    head = 2 * t + half

    def out_att(d, s):
        to = (t + d) % TILE_DEV
        return remote(
            att_st.at[:, s, to], att_in.at[head], att_send.at[2 * d + s], att_recv.at[head], to,
            partner if s else b,
        )

    def from_att(d, s):
        src = (t + d) % TILE_DEV
        other = 2 * src + (1 - half if s else half)
        return remote(
            att_st.at[:, s, 0], att_in.at[other], att_send.at[0], att_recv.at[other], src, partner if s else b
        )

    pairs = [(d, s) for d in range(TILE_DEV) for s in range(2) if d + s]
    for d, s in pairs:
        out_att(d, s).start()
    att_in[head] = att_st[:, 0, t]
    for d in range(1, 4):
        out_x(d).wait_send()
    for i in range(2):
        out_z(i).wait_send()
    for c in range(CHUNKS):
        for d in range(1, TILE_DEV):
            out_emb(c, d).wait_send()
        for i in range(4):
            out_kv(c, i, False).wait_send()
            if i:
                out_kv(c, i, True).wait_send()
        pass_on(c).wait_send()
        swap_q(c).wait_send()
    out_core().wait_send()
    from_core().wait_recv()
    for d, s in pairs:
        from_att(d, s).wait_recv()
    attended = jnp.concatenate([att_in[2 * k + p].reshape(PER_DEV, 128)[:, 0:HD] for p in range(2) for k in range(TILE_DEV)], axis=1)
    mixed = jnp.dot(attended, wo[...].reshape(E, E), preferred_element_type=F32)
    o_ref[...] = (emb[...].reshape(PER_DEV, E).astype(F32) + mixed).astype(BF)

    for d, s in pairs:
        out_att(d, s).wait_send()


def shards(
    tiles, w_reduce, w_spatial, w_expand, w_embed, w_query, w_key, w_value, w_out, slide_tiles
):
    anywhere = pl.BlockSpec(memory_space=pl.ANY)
    dma = pltpu.SemaphoreType.DMA
    vmem = pltpu.VMEM
    width = 2 * HD
    return pl.pallas_call(
        body,
        in_specs=[pl.BlockSpec(memory_space=pltpu.SMEM)] + [anywhere] * 9,
        out_specs=pl.BlockSpec(memory_space=vmem),
        out_shape=jax.ShapeDtypeStruct((PER_DEV, E), BF),
        scratch_shapes=[
            vmem((2, T, 8, 8, C), BF),
            vmem((C, MID), BF),
            vmem((3, 3 * MID, MID), BF),
            vmem((MID, C), BF),
            vmem((C, E), BF),
            vmem((3, width, E), BF),
            vmem((2, TILE_DEV, HD, E), BF),
            vmem((T, 10, 8, 3 * MID), BF),
            vmem((T, C), BF),
            vmem((CHUNKS, T, E), BF),
            vmem((CHUNKS, TILE_DEV, T, E), BF),
            vmem((CHUNKS, HD, LANES), BF),
            vmem((CHUNKS, 2, width, LANES), BF),
            vmem((CHUNKS, HD, QW), BF),
            vmem((CHUNKS, width, SLOTS * LANES), BF),
            vmem((CHUNKS * SLOTS * LANES, 128), jnp.int32),
            vmem((1, CHUNKS * QW), F32),
            vmem((1, CHUNKS * QW), F32),
            vmem((HD, CHUNKS * QW), F32),
            vmem((CHUNKS, 2, TILE_DEV, T, 128), BF),
            vmem((HEADS, CHUNKS, T, 128), BF),
            dma((2,)), dma((7,)), dma,
            dma((CHUNKS, 8)), dma((CHUNKS, 8)),
            dma((CHUNKS, 16)), dma((CHUNKS, 16)),
            dma((CHUNKS,)), dma((CHUNKS,)),
            dma((16,)), dma((16,)),
            dma((16,)), dma((16,)),
        ],
        compiler_params=pltpu.CompilerParams(
            vmem_limit_bytes=VMEM_LIMIT, collective_id=0, has_side_effects=True
        ),
        name="slide_step",
    )(
        slide_tiles, tiles, w_reduce, w_spatial.reshape(3, 3 * MID, MID), w_expand, w_embed,
        w_query.T, w_key.T, w_value.T, w_out,
    )


def solution(mesh):
    placed = (
        P(("blk", "tile"), None, None, None),
        P(),
        P(),
        P(),
        P(),
        P(None, "tile"),
        P(None, "tile"),
        P(None, "tile"),
        P("tile", None),
        P(),
    )
    return jax.shard_map(
        shards, mesh=mesh, in_specs=placed, out_specs=P(("blk", "tile"), None), check_vma=False
    )
```

```python
import math

import jax
import jax.numpy as jnp
from jax import lax
from jax.experimental import pallas as pl
from jax.experimental.pallas import tpu as pltpu
from jax.sharding import PartitionSpec as P

C = 2048
MID = 512
HD = 96
E = 1536
HEADS = 16
TILE_DEV = 8
PER_DEV = 48
T = 16
CHUNKS = PER_DEV // T
R = T * 64
LANES = T * TILE_DEV
SHARD = PER_DEV * TILE_DEV
SLOTS = 16
QW = 2 * LANES
NEG = -1e30
RATE = 1.4426950408889634 / math.sqrt(HD)
VMEM_LIMIT = 61 << 20
MESH = pl.DeviceIdType.MESH
BF = jnp.bfloat16
F32 = jnp.float32


def normalize(rows):
    values = rows.astype(F32)
    center = jnp.mean(values, axis=1, keepdims=True)
    spread = jnp.mean((values - center) ** 2, axis=1, keepdims=True)
    return ((values - center) * lax.rsqrt(spread + 1e-05)).astype(BF)


def nt(a, b):
    return lax.dot_general(a, b, (((1,), (1,)), ((), ())), preferred_element_type=F32)


def body(
    slides, tiles, wr_hbm, ws_hbm, wx_hbm, we_hbm, wq_hbm, wk_hbm, wv_hbm, wo_hbm, o_ref,
    x_buf, wr, ws, wx, we, wqkv, wo, near, pool, emb, emb_all, q_st, kv_st, q_all, kv_all,
    key_slide, top, total, acc, att_st, att_in,
    x_sem, w_sem, own_sem, emb_send, emb_recv, kv_send, kv_recv, q_send, q_recv, att_send, att_recv,
    wo_send, wo_recv,
):
    t = lax.axis_index("tile")
    b = lax.axis_index("blk")
    core = b % 2
    half = (b // 2) % 2
    y = b // 4
    partner = b + 2 - 4 * half
    sibling = b + 1 - 2 * core
    x = t % 4
    z_lo = t // 4
    mine = 2 * y + half

    def remote(src, dst, send, recv, tile, blk):
        return pltpu.make_async_remote_copy(
            src_ref=src, dst_ref=dst, send_sem=send, recv_sem=recv,
            device_id={"tile": tile, "blk": blk}, device_id_type=MESH,
        )

    def load_x(c):
        return pltpu.make_async_copy(tiles.at[pl.ds(c * T, T)], x_buf.at[c % 2], x_sem.at[c % 2])

    weights = [
        pltpu.make_async_copy(a, v, w_sem.at[i])
        for i, (a, v) in enumerate(
            zip((wr_hbm, ws_hbm, wx_hbm, we_hbm, wk_hbm, wv_hbm, wq_hbm), (wr, ws, wx, we, wqkv.at[0], wqkv.at[1], wqkv.at[2]))
        )
    ]
    load_x(0).start()
    for copy in weights:
        copy.start()

    own_rows = pltpu.make_async_copy(wo_hbm.at[pl.ds(core * HD, HD)], wo.at[core, t], own_sem)

    def out_x(d):
        rows = wo_hbm.at[pl.ds(core * HD, HD)]
        return remote(rows, wo.at[core, t], wo_send.at[d], wo_recv.at[x], z_lo * 4 + (x + d) % 4, b)

    def from_x(d):
        src = (x + d) % 4
        there = wo.at[core, z_lo * 4 + src]
        return remote(there, there, wo_send.at[0], wo_recv.at[src], z_lo * 4 + src, b)

    z = 2 * half + z_lo

    def out_z(i):
        to = (z + (3 if i else 1)) % 4
        rows = wo.at[core, pl.ds(z_lo * 4 + 2 * i, 2)]
        return remote(
            rows, rows, wo_send.at[4 + i], wo_recv.at[4 + i],
            (to % 2) * 4 + x, y * 4 + (to // 2) * 2 + core,
        )

    def from_z(i):
        src = (z + (1 if i else 3)) % 4
        rows = wo.at[core, pl.ds((1 - z_lo) * 4 + 2 * i, 2)]
        return remote(
            rows, rows, wo_send.at[0], wo_recv.at[4 + i],
            (src % 2) * 4 + x, y * 4 + (src // 2) * 2 + core,
        )

    def out_core():
        return remote(wo.at[core], wo.at[core], wo_send.at[6], wo_recv.at[6], t, sibling)

    def from_core():
        return remote(wo.at[1 - core], wo.at[1 - core], wo_send.at[6], wo_recv.at[6], t, sibling)

    def out_emb(c, d):
        return remote(
            emb.at[c], emb_all.at[c, t], emb_send.at[c, d], emb_recv.at[c, t], (t + d) % TILE_DEV, b
        )

    def from_emb(c, d):
        src = (t + d) % TILE_DEV
        return remote(emb.at[c], emb_all.at[c, src], emb_send.at[c, d], emb_recv.at[c, src], src, b)

    def slot_of(c, s):
        return kv_all.at[c, s]

    def out_kv(c, i, same):
        to = ((y + i) % 4) * 4 + core + 2 * (half if same else 1 - half)
        return remote(
            kv_st.at[c, half if same else 1 - half], slot_of(c, mine),
            kv_send.at[c, 2 * i + (0 if same else 1)], kv_recv.at[c, mine], t, to,
        )

    def from_kv(c, d):
        u = (mine + d) % 8
        return remote(
            kv_st.at[c, 0], slot_of(c, u), kv_send.at[c, 0], kv_recv.at[c, u], t, 2 * u + core
        )

    def pass_on(c):
        return remote(
            kv_all.at[c, 0:8], kv_all.at[c, 8:16], kv_send.at[c, 8], kv_recv.at[c, 8], t, sibling
        )

    def swap_q(c):
        return remote(
            q_st.at[c], q_all.at[c, :, LANES:QW], q_send.at[c], q_recv.at[c], t, partner
        )

    barrier = pltpu.get_barrier_semaphore()
    for d in range(1, TILE_DEV):
        for blk in (b, partner):
            pl.semaphore_signal(
                barrier, inc=1, device_id={"tile": (t + d) % TILE_DEV, "blk": blk}, device_id_type=MESH
            )
    for d in range(1, 8):
        pl.semaphore_signal(
            barrier, inc=1, device_id={"tile": t, "blk": 2 * ((mine + d) % 8) + core}, device_id_type=MESH
        )
    pl.semaphore_signal(barrier, inc=1, device_id={"tile": t, "blk": sibling}, device_id_type=MESH)

    near[:, 0] = jnp.zeros((T, 8, 3 * MID), BF)
    near[:, 9] = jnp.zeros((T, 8, 3 * MID), BF)
    own_rows.start()

    pl.semaphore_wait(barrier, 2 * (TILE_DEV - 1) + 8)
    for d in range(1, 4):
        out_x(d).start()

    ends = [slides[0], slides[0] + slides[1], slides[0] + slides[1] + slides[2]]

    def slide_at(pos):
        return sum((pos >= end).astype(jnp.int32) for end in ends)

    def table(i, carry):
        n = lax.broadcasted_iota(jnp.int32, (512, 128), 0) + 512 * (i % 4)
        slot = n >> 7
        blk = 2 * (slot & 7) + jnp.where(slot < 8, core, 1 - core)
        pos = blk * SHARD + ((n >> 4) & 7) * PER_DEV + (i // 4) * T + (n & 15)
        key_slide[pl.ds(pl.multiple_of(i * 512, 512), 512), :] = slide_at(pos)
        return carry

    n = lax.broadcasted_iota(jnp.int32, (8, CHUNKS * QW), 1)
    query_pos = (
        jnp.where(((n >> 7) & 1) == 0, b, partner) * SHARD + ((n >> 4) & 7) * PER_DEV + (n >> 8) * T + (n & 15)
    )
    query_slide = slide_at(query_pos)[0:1]
    top[...] = jnp.full((1, CHUNKS * QW), NEG, F32)
    total[...] = jnp.zeros((1, CHUNKS * QW), F32)
    acc[...] = jnp.zeros((HD, CHUNKS * QW), F32)

    lax.fori_loop(0, 12, table, 0)

    def project(c):
        for d in range(1, TILE_DEV):
            from_emb(c, d).wait_recv()
        normed = normalize(emb_all[c].reshape(LANES, E))
        joined = nt(wqkv[...].reshape(6 * HD, E), normed).astype(BF)
        for h in range(2):
            kv_st[c, h, 0:HD] = joined[h * HD : (h + 1) * HD]
            kv_st[c, h, HD : 2 * HD] = joined[(2 + h) * HD : (3 + h) * HD]
        for i in range(4):
            out_kv(c, i, False).start()
            if i:
                out_kv(c, i, True).start()
        kv_all[c, mine] = kv_st[c, half]
        first, second = joined[4 * HD : 5 * HD], joined[5 * HD : 6 * HD]
        q_all[c, :, 0:LANES] = jnp.where(half == 0, first, second)
        q_st[c] = jnp.where(half == 0, second, first)
        swap_q(c).start()

    def relay(c):
        for d in range(1, 8):
            from_kv(c, d).wait_recv()
        pass_on(c).start()

    def attend(c, group, first, last):
        lanes = slice(first * QW, last * QW)
        key = jnp.concatenate([kv_all[c, group * 8 + k, 0:HD] for k in range(8)], axis=1).T
        value = jnp.concatenate([kv_all[c, group * 8 + k, HD : 2 * HD] for k in range(8)], axis=1)
        query = jnp.concatenate([q_all[i] for i in range(first, last)], axis=1)
        scores = jnp.dot(key, query, preferred_element_type=F32) * RATE
        slide = key_slide[pl.ds(pl.multiple_of(c * 2048 + group * 1024, 1024), 1024), :]
        slide = jnp.concatenate([slide] * ((last - first) * 2), axis=1)
        scores = jnp.where(slide == query_slide[:, lanes], scores, NEG)
        old = top[:, lanes]
        new = jnp.maximum(old, jnp.max(scores, axis=0, keepdims=True))
        weights = jnp.exp2(scores - new)
        keep = jnp.exp2(old - new)
        top[:, lanes] = new
        total[:, lanes] = total[:, lanes] * keep + jnp.sum(weights, axis=0, keepdims=True)
        acc[:, lanes] = acc[:, lanes] * keep + jnp.dot(
            value, weights.astype(BF), preferred_element_type=F32
        )

    def encode(c, carry):
        load_x(c).wait()

        @pl.when(c < CHUNKS - 1)
        def _():
            load_x(c + 1).start()

        def first_use(i):
            @pl.when(c == 0)
            def _():
                weights[i].wait()

        first_use(0)
        x_ref = x_buf.at[c % 2]
        r = jnp.maximum(jnp.dot(x_ref[...].reshape(R, C), wr[...], preferred_element_type=F32), 0.0)
        j = lax.broadcasted_iota(jnp.int32, (R, MID), 0) % 8
        left = jnp.where(j == 0, 0.0, pltpu.roll(r, 1, 0))
        right = jnp.where(j == 7, 0.0, pltpu.roll(r, R - 1, 0))
        for at, shifted in enumerate((left, r, right)):
            near[:, 1:9, :, at * MID : (at + 1) * MID] = shifted.astype(BF).reshape(T, 8, 8, MID)
        first_use(1)
        conv = sum(
            jnp.dot(near[:, k : k + 8].reshape(R, 3 * MID), ws[k], preferred_element_type=F32) for k in range(3)
        )
        s = jnp.maximum(conv, 0.0).astype(BF)
        first_use(2)

        @pl.when(c > 0)
        def _():
            project(c - 1)

        @pl.when(c == 1)
        def _():
            for d in range(1, 4):
                from_x(d).wait_recv()
            for i in range(2):
                out_z(i).start()

        for k in range(4):
            cols = slice(k * 512, (k + 1) * 512)
            out = jnp.dot(s, wx[:, cols], preferred_element_type=F32)
            out = jnp.maximum(out + x_ref[:, :, :, cols].reshape(R, 512).astype(F32), 0.0)
            pool[:, cols] = (jnp.sum(jnp.sum(out.reshape(T, 8, 8, 512), axis=1), axis=1) * (1.0 / 64)).astype(BF)
        first_use(3)
        emb[c] = jnp.dot(pool[...], we[...], preferred_element_type=F32).astype(BF)
        for d in range(1, TILE_DEV):
            out_emb(c, d).start()
        emb_all[c, t] = emb[c]

        @pl.when(c == 0)
        def _():
            for i in range(4, 7):
                weights[i].wait()
            own_rows.wait()

        @pl.when(c > 0)
        def _():
            relay(c - 1)

        return carry

    lax.fori_loop(0, CHUNKS, encode, 0)

    def sweep(c, first, last, start=0, stop=2):
        def block(g, carry):
            attend(c, g, first, last)
            return carry

        lax.fori_loop(start, stop, block, 0)

    for c in range(2):
        swap_q(c).wait_recv()
    for c in range(2):
        pass_on(c).wait_recv()
        sweep(c, 0, 2)
    project(2)
    swap_q(2).wait_recv()
    sweep(0, 2, 3)
    relay(2)
    sweep(1, 2, 3)
    for i in range(2):
        from_z(i).wait_recv()
    out_core().start()
    attend(2, 0, 0, 3)
    pass_on(2).wait_recv()
    attend(2, 1, 0, 3)

    result = (acc[...] / total[...]).T.astype(BF)
    att_st[...] = jnp.concatenate(
        [result, jnp.zeros((CHUNKS * QW, 128 - HD), BF)], axis=1
    ).reshape(CHUNKS, 2, TILE_DEV, T, 128)
    head = 2 * t + half

    def out_att(d, s):
        to = (t + d) % TILE_DEV
        return remote(
            att_st.at[:, s, to], att_in.at[head], att_send.at[2 * d + s], att_recv.at[head], to,
            partner if s else b,
        )

    def from_att(d, s):
        src = (t + d) % TILE_DEV
        other = 2 * src + (1 - half if s else half)
        return remote(
            att_st.at[:, s, 0], att_in.at[other], att_send.at[0], att_recv.at[other], src, partner if s else b
        )

    pairs = [(d, s) for d in range(TILE_DEV) for s in range(2) if d + s]
    for d, s in pairs:
        out_att(d, s).start()
    att_in[head] = att_st[:, 0, t]
    for d in range(1, 4):
        out_x(d).wait_send()
    for i in range(2):
        out_z(i).wait_send()
    for c in range(CHUNKS):
        for d in range(1, TILE_DEV):
            out_emb(c, d).wait_send()
        for i in range(4):
            out_kv(c, i, False).wait_send()
            if i:
                out_kv(c, i, True).wait_send()
        pass_on(c).wait_send()
        swap_q(c).wait_send()
    out_core().wait_send()
    from_core().wait_recv()
    for d, s in pairs:
        from_att(d, s).wait_recv()
    attended = jnp.concatenate([att_in[2 * k + p].reshape(PER_DEV, 128)[:, 0:HD] for p in range(2) for k in range(TILE_DEV)], axis=1)
    mixed = jnp.dot(attended, wo[...].reshape(E, E), preferred_element_type=F32)
    o_ref[...] = (emb[...].reshape(PER_DEV, E).astype(F32) + mixed).astype(BF)

    for d, s in pairs:
        out_att(d, s).wait_send()


def shards(
    tiles, w_reduce, w_spatial, w_expand, w_embed, w_query, w_key, w_value, w_out, slide_tiles
):
    anywhere = pl.BlockSpec(memory_space=pl.ANY)
    dma = pltpu.SemaphoreType.DMA
    vmem = pltpu.VMEM
    width = 2 * HD
    return pl.pallas_call(
        body,
        in_specs=[pl.BlockSpec(memory_space=pltpu.SMEM)] + [anywhere] * 9,
        out_specs=pl.BlockSpec(memory_space=vmem),
        out_shape=jax.ShapeDtypeStruct((PER_DEV, E), BF),
        scratch_shapes=[
            vmem((2, T, 8, 8, C), BF),
            vmem((C, MID), BF),
            vmem((3, 3 * MID, MID), BF),
            vmem((MID, C), BF),
            vmem((C, E), BF),
            vmem((3, width, E), BF),
            vmem((2, TILE_DEV, HD, E), BF),
            vmem((T, 10, 8, 3 * MID), BF),
            vmem((T, C), BF),
            vmem((CHUNKS, T, E), BF),
            vmem((CHUNKS, TILE_DEV, T, E), BF),
            vmem((CHUNKS, HD, LANES), BF),
            vmem((CHUNKS, 2, width, LANES), BF),
            vmem((CHUNKS, HD, QW), BF),
            vmem((CHUNKS, SLOTS, width, LANES), BF),
            vmem((CHUNKS * SLOTS * LANES, 128), jnp.int32),
            vmem((1, CHUNKS * QW), F32),
            vmem((1, CHUNKS * QW), F32),
            vmem((HD, CHUNKS * QW), F32),
            vmem((CHUNKS, 2, TILE_DEV, T, 128), BF),
            vmem((HEADS, CHUNKS, T, 128), BF),
            dma((2,)), dma((7,)), dma,
            dma((CHUNKS, 8)), dma((CHUNKS, 8)),
            dma((CHUNKS, 16)), dma((CHUNKS, 16)),
            dma((CHUNKS,)), dma((CHUNKS,)),
            dma((16,)), dma((16,)),
            dma((16,)), dma((16,)),
        ],
        compiler_params=pltpu.CompilerParams(
            vmem_limit_bytes=VMEM_LIMIT, collective_id=0, has_side_effects=True
        ),
        name="slide_step",
    )(
        slide_tiles, tiles, w_reduce, w_spatial.reshape(3, 3 * MID, MID), w_expand, w_embed,
        w_query.T, w_key.T, w_value.T, w_out,
    )


def solution(mesh):
    placed = (
        P(("blk", "tile"), None, None, None),
        P(),
        P(),
        P(),
        P(),
        P(None, "tile"),
        P(None, "tile"),
        P(None, "tile"),
        P("tile", None),
        P(),
    )
    return jax.shard_map(
        shards, mesh=mesh, in_specs=placed, out_specs=P(("blk", "tile"), None), check_vma=False
    )
```

```python
import math

import jax
import jax.numpy as jnp
from jax import lax
from jax.experimental import pallas as pl
from jax.experimental.pallas import tpu as pltpu
from jax.sharding import PartitionSpec as P

C = 2048
MID = 512
HD = 96
E = 1536
HEADS = 16
TILE_DEV = 8
PER_DEV = 48
T = 16
CHUNKS = PER_DEV // T
R = T * 64
LANES = T * TILE_DEV
SHARD = PER_DEV * TILE_DEV
SLOTS = 16
QW = 2 * LANES
NEG = -1e30
RATE = 1.4426950408889634 / math.sqrt(HD)
VMEM_LIMIT = 61 << 20
MESH = pl.DeviceIdType.MESH
BF = jnp.bfloat16
F32 = jnp.float32


def normalize(rows):
    values = rows.astype(F32)
    center = jnp.mean(values, axis=1, keepdims=True)
    spread = jnp.mean((values - center) ** 2, axis=1, keepdims=True)
    return ((values - center) * lax.rsqrt(spread + 1e-05)).astype(BF)


def nt(a, b):
    return lax.dot_general(a, b, (((1,), (1,)), ((), ())), preferred_element_type=F32)


def body(
    slides, tiles, wr_hbm, ws_hbm, wx_hbm, we_hbm, wq_hbm, wk_hbm, wv_hbm, wo_hbm, o_ref,
    x_buf, wr, ws, wx, we, wqkv, wo, near, pool, emb, emb_all, q_st, kv_st, q_all, kv_all,
    key_slide, top, total, acc, att_st, att_in,
    x_sem, w_sem, own_sem, emb_send, emb_recv, kv_send, kv_recv, q_send, q_recv, att_send, att_recv,
    wo_send, wo_recv,
):
    t = lax.axis_index("tile")
    b = lax.axis_index("blk")
    core = b % 2
    half = (b // 2) % 2
    y = b // 4
    partner = b + 2 - 4 * half
    sibling = b + 1 - 2 * core
    x = t % 4
    z_lo = t // 4
    mine = 2 * y + half

    def remote(src, dst, send, recv, tile, blk):
        return pltpu.make_async_remote_copy(
            src_ref=src, dst_ref=dst, send_sem=send, recv_sem=recv,
            device_id={"tile": tile, "blk": blk}, device_id_type=MESH,
        )

    def load_x(c):
        return pltpu.make_async_copy(tiles.at[pl.ds(c * T, T)], x_buf.at[c % 2], x_sem.at[c % 2])

    weights = [
        pltpu.make_async_copy(a, v, w_sem.at[i])
        for i, (a, v) in enumerate(
            zip((wr_hbm, ws_hbm, wx_hbm, we_hbm, wk_hbm, wv_hbm, wq_hbm), (wr, ws, wx, we, wqkv.at[0], wqkv.at[1], wqkv.at[2]))
        )
    ]
    load_x(0).start()
    for copy in weights:
        copy.start()

    own_rows = pltpu.make_async_copy(wo_hbm.at[pl.ds(core * HD, HD)], wo.at[core, t], own_sem)

    def out_x(d):
        rows = wo_hbm.at[pl.ds(core * HD, HD)]
        return remote(rows, wo.at[core, t], wo_send.at[d], wo_recv.at[x], z_lo * 4 + (x + d) % 4, b)

    def from_x(d):
        src = (x + d) % 4
        there = wo.at[core, z_lo * 4 + src]
        return remote(there, there, wo_send.at[0], wo_recv.at[src], z_lo * 4 + src, b)

    def over_x(i):
        src = z_lo * 4 + (x + (1 if i else 3)) % 4
        rows = wo.at[core, src, pl.ds(48 * i, 48)]
        return remote(
            rows, rows, wo_send.at[7 + i], wo_recv.at[7 + i], z_lo * 4 + (x + (3 if i else 1)) % 4, b
        )

    def from_over_x(i):
        rows = wo.at[core, z_lo * 4 + (x + 2) % 4, pl.ds(48 * i, 48)]
        return remote(
            rows, rows, wo_send.at[0], wo_recv.at[7 + i], z_lo * 4 + (x + (1 if i else 3)) % 4, b
        )

    z = 2 * half + z_lo

    def out_z(i):
        to = (z + (3 if i else 1)) % 4
        rows = wo.at[core, pl.ds(z_lo * 4 + 2 * i, 2)]
        return remote(
            rows, rows, wo_send.at[4 + i], wo_recv.at[4 + i],
            (to % 2) * 4 + x, y * 4 + (to // 2) * 2 + core,
        )

    def from_z(i):
        src = (z + (1 if i else 3)) % 4
        rows = wo.at[core, pl.ds((1 - z_lo) * 4 + 2 * i, 2)]
        return remote(
            rows, rows, wo_send.at[0], wo_recv.at[4 + i],
            (src % 2) * 4 + x, y * 4 + (src // 2) * 2 + core,
        )

    def out_core():
        return remote(wo.at[core], wo.at[core], wo_send.at[6], wo_recv.at[6], t, sibling)

    def from_core():
        return remote(wo.at[1 - core], wo.at[1 - core], wo_send.at[6], wo_recv.at[6], t, sibling)

    def out_emb(c, d):
        return remote(
            emb.at[c], emb_all.at[c, t], emb_send.at[c, d], emb_recv.at[c, t], (t + d) % TILE_DEV, b
        )

    def from_emb(c, d):
        src = (t + d) % TILE_DEV
        return remote(emb.at[c], emb_all.at[c, src], emb_send.at[c, d], emb_recv.at[c, src], src, b)

    def slot_of(c, s):
        return kv_all.at[c, s]

    def out_kv(c, i, same):
        to = ((y + i) % 4) * 4 + core + 2 * (half if same else 1 - half)
        return remote(
            kv_st.at[c, half if same else 1 - half], slot_of(c, mine),
            kv_send.at[c, 2 * i + (0 if same else 1)], kv_recv.at[c, mine], t, to,
        )

    def from_kv(c, d):
        u = (mine + d) % 8
        return remote(
            kv_st.at[c, 0], slot_of(c, u), kv_send.at[c, 0], kv_recv.at[c, u], t, 2 * u + core
        )

    def pass_on(c):
        return remote(
            kv_all.at[c, 0:8], kv_all.at[c, 8:16], kv_send.at[c, 8], kv_recv.at[c, 8], t, sibling
        )

    def swap_q(c):
        return remote(
            q_st.at[c], q_all.at[c, :, LANES:QW], q_send.at[c], q_recv.at[c], t, partner
        )

    barrier = pltpu.get_barrier_semaphore()
    for d in range(1, TILE_DEV):
        for blk in (b, partner):
            pl.semaphore_signal(
                barrier, inc=1, device_id={"tile": (t + d) % TILE_DEV, "blk": blk}, device_id_type=MESH
            )
    for d in range(1, 8):
        pl.semaphore_signal(
            barrier, inc=1, device_id={"tile": t, "blk": 2 * ((mine + d) % 8) + core}, device_id_type=MESH
        )
    pl.semaphore_signal(barrier, inc=1, device_id={"tile": t, "blk": sibling}, device_id_type=MESH)

    near[:, 0] = jnp.zeros((T, 8, 3 * MID), BF)
    near[:, 9] = jnp.zeros((T, 8, 3 * MID), BF)
    own_rows.start()

    pl.semaphore_wait(barrier, 2 * (TILE_DEV - 1) + 8)
    for d in (1, 3):
        out_x(d).start()

    ends = [slides[0], slides[0] + slides[1], slides[0] + slides[1] + slides[2]]

    def slide_at(pos):
        return sum((pos >= end).astype(jnp.int32) for end in ends)

    def table(i, carry):
        n = lax.broadcasted_iota(jnp.int32, (512, 128), 0) + 512 * (i % 4)
        slot = n >> 7
        blk = 2 * (slot & 7) + jnp.where(slot < 8, core, 1 - core)
        pos = blk * SHARD + ((n >> 4) & 7) * PER_DEV + (i // 4) * T + (n & 15)
        key_slide[pl.ds(pl.multiple_of(i * 512, 512), 512), :] = slide_at(pos)
        return carry

    n = lax.broadcasted_iota(jnp.int32, (8, CHUNKS * QW), 1)
    query_pos = (
        jnp.where(((n >> 7) & 1) == 0, b, partner) * SHARD + ((n >> 4) & 7) * PER_DEV + (n >> 8) * T + (n & 15)
    )
    query_slide = slide_at(query_pos)[0:1]
    top[...] = jnp.full((1, CHUNKS * QW), NEG, F32)
    total[...] = jnp.zeros((1, CHUNKS * QW), F32)
    acc[...] = jnp.zeros((HD, CHUNKS * QW), F32)

    lax.fori_loop(0, 12, table, 0)

    def project(c):
        for d in range(1, TILE_DEV):
            from_emb(c, d).wait_recv()
        normed = normalize(emb_all[c].reshape(LANES, E))
        joined = nt(wqkv[...].reshape(6 * HD, E), normed).astype(BF)
        for h in range(2):
            kv_st[c, h, 0:HD] = joined[h * HD : (h + 1) * HD]
            kv_st[c, h, HD : 2 * HD] = joined[(2 + h) * HD : (3 + h) * HD]
        for i in range(4):
            out_kv(c, i, False).start()
            if i:
                out_kv(c, i, True).start()
        kv_all[c, mine] = kv_st[c, half]
        first, second = joined[4 * HD : 5 * HD], joined[5 * HD : 6 * HD]
        q_all[c, :, 0:LANES] = jnp.where(half == 0, first, second)
        q_st[c] = jnp.where(half == 0, second, first)
        swap_q(c).start()

    def relay(c):
        for d in range(1, 8):
            from_kv(c, d).wait_recv()
        pass_on(c).start()

    def attend(c, group, first, last):
        lanes = slice(first * QW, last * QW)
        key = jnp.concatenate([kv_all[c, group * 8 + k, 0:HD] for k in range(8)], axis=1).T
        value = jnp.concatenate([kv_all[c, group * 8 + k, HD : 2 * HD] for k in range(8)], axis=1)
        query = jnp.concatenate([q_all[i] for i in range(first, last)], axis=1)
        scores = jnp.dot(key, query, preferred_element_type=F32) * RATE
        slide = key_slide[pl.ds(pl.multiple_of(c * 2048 + group * 1024, 1024), 1024), :]
        slide = jnp.concatenate([slide] * ((last - first) * 2), axis=1)
        scores = jnp.where(slide == query_slide[:, lanes], scores, NEG)
        old = top[:, lanes]
        new = jnp.maximum(old, jnp.max(scores, axis=0, keepdims=True))
        weights = jnp.exp2(scores - new)
        keep = jnp.exp2(old - new)
        top[:, lanes] = new
        total[:, lanes] = total[:, lanes] * keep + jnp.sum(weights, axis=0, keepdims=True)
        acc[:, lanes] = acc[:, lanes] * keep + jnp.dot(
            value, weights.astype(BF), preferred_element_type=F32
        )

    def encode(c, carry):
        load_x(c).wait()

        @pl.when(c < CHUNKS - 1)
        def _():
            load_x(c + 1).start()

        def first_use(i):
            @pl.when(c == 0)
            def _():
                weights[i].wait()

        first_use(0)
        x_ref = x_buf.at[c % 2]
        r = jnp.maximum(jnp.dot(x_ref[...].reshape(R, C), wr[...], preferred_element_type=F32), 0.0)
        j = lax.broadcasted_iota(jnp.int32, (R, MID), 0) % 8
        left = jnp.where(j == 0, 0.0, pltpu.roll(r, 1, 0))
        right = jnp.where(j == 7, 0.0, pltpu.roll(r, R - 1, 0))
        for at, shifted in enumerate((left, r, right)):
            near[:, 1:9, :, at * MID : (at + 1) * MID] = shifted.astype(BF).reshape(T, 8, 8, MID)
        first_use(1)
        conv = sum(
            jnp.dot(near[:, k : k + 8].reshape(R, 3 * MID), ws[k], preferred_element_type=F32) for k in range(3)
        )
        s = jnp.maximum(conv, 0.0).astype(BF)
        first_use(2)

        @pl.when(c == 0)
        def _():
            for d in (1, 3):
                from_x(d).wait_recv()
            for i in range(2):
                over_x(i).start()

        @pl.when(c > 0)
        def _():
            project(c - 1)

        @pl.when(c == 1)
        def _():
            for i in range(2):
                from_over_x(i).wait_recv()
            for i in range(2):
                out_z(i).start()

        for k in range(4):
            cols = slice(k * 512, (k + 1) * 512)
            out = jnp.dot(s, wx[:, cols], preferred_element_type=F32)
            out = jnp.maximum(out + x_ref[:, :, :, cols].reshape(R, 512).astype(F32), 0.0)
            pool[:, cols] = (jnp.sum(jnp.sum(out.reshape(T, 8, 8, 512), axis=1), axis=1) * (1.0 / 64)).astype(BF)
        first_use(3)
        emb[c] = jnp.dot(pool[...], we[...], preferred_element_type=F32).astype(BF)
        for d in range(1, TILE_DEV):
            out_emb(c, d).start()
        emb_all[c, t] = emb[c]

        @pl.when(c == 0)
        def _():
            for i in range(4, 7):
                weights[i].wait()
            own_rows.wait()

        @pl.when(c > 0)
        def _():
            relay(c - 1)

        return carry

    lax.fori_loop(0, CHUNKS, encode, 0)

    def sweep(c, first, last, start=0, stop=2):
        def block(g, carry):
            attend(c, g, first, last)
            return carry

        lax.fori_loop(start, stop, block, 0)

    for c in range(2):
        swap_q(c).wait_recv()
    for c in range(2):
        pass_on(c).wait_recv()
        sweep(c, 0, 2)
    project(2)
    swap_q(2).wait_recv()
    sweep(0, 2, 3)
    relay(2)
    sweep(1, 2, 3)
    for i in range(2):
        from_z(i).wait_recv()
    out_core().start()
    attend(2, 0, 0, 3)
    pass_on(2).wait_recv()
    attend(2, 1, 0, 3)

    result = (acc[...] / total[...]).T.astype(BF)
    att_st[...] = jnp.concatenate(
        [result, jnp.zeros((CHUNKS * QW, 128 - HD), BF)], axis=1
    ).reshape(CHUNKS, 2, TILE_DEV, T, 128)
    head = 2 * t + half

    def out_att(d, s):
        to = (t + d) % TILE_DEV
        return remote(
            att_st.at[:, s, to], att_in.at[head], att_send.at[2 * d + s], att_recv.at[head], to,
            partner if s else b,
        )

    def from_att(d, s):
        src = (t + d) % TILE_DEV
        other = 2 * src + (1 - half if s else half)
        return remote(
            att_st.at[:, s, 0], att_in.at[other], att_send.at[0], att_recv.at[other], src, partner if s else b
        )

    pairs = [(d, s) for d in range(TILE_DEV) for s in range(2) if d + s]
    for d, s in pairs:
        out_att(d, s).start()
    att_in[head] = att_st[:, 0, t]
    for d in (1, 3):
        out_x(d).wait_send()
    for i in range(2):
        over_x(i).wait_send()
        out_z(i).wait_send()
    for c in range(CHUNKS):
        for d in range(1, TILE_DEV):
            out_emb(c, d).wait_send()
        for i in range(4):
            out_kv(c, i, False).wait_send()
            if i:
                out_kv(c, i, True).wait_send()
        pass_on(c).wait_send()
        swap_q(c).wait_send()
    out_core().wait_send()
    from_core().wait_recv()
    for d, s in pairs:
        from_att(d, s).wait_recv()
    attended = jnp.concatenate([att_in[2 * k + p].reshape(PER_DEV, 128)[:, 0:HD] for p in range(2) for k in range(TILE_DEV)], axis=1)
    mixed = jnp.dot(attended, wo[...].reshape(E, E), preferred_element_type=F32)
    o_ref[...] = (emb[...].reshape(PER_DEV, E).astype(F32) + mixed).astype(BF)

    for d, s in pairs:
        out_att(d, s).wait_send()


def shards(
    tiles, w_reduce, w_spatial, w_expand, w_embed, w_query, w_key, w_value, w_out, slide_tiles
):
    anywhere = pl.BlockSpec(memory_space=pl.ANY)
    dma = pltpu.SemaphoreType.DMA
    vmem = pltpu.VMEM
    width = 2 * HD
    return pl.pallas_call(
        body,
        in_specs=[pl.BlockSpec(memory_space=pltpu.SMEM)] + [anywhere] * 9,
        out_specs=pl.BlockSpec(memory_space=vmem),
        out_shape=jax.ShapeDtypeStruct((PER_DEV, E), BF),
        scratch_shapes=[
            vmem((2, T, 8, 8, C), BF),
            vmem((C, MID), BF),
            vmem((3, 3 * MID, MID), BF),
            vmem((MID, C), BF),
            vmem((C, E), BF),
            vmem((3, width, E), BF),
            vmem((2, TILE_DEV, HD, E), BF),
            vmem((T, 10, 8, 3 * MID), BF),
            vmem((T, C), BF),
            vmem((CHUNKS, T, E), BF),
            vmem((CHUNKS, TILE_DEV, T, E), BF),
            vmem((CHUNKS, HD, LANES), BF),
            vmem((CHUNKS, 2, width, LANES), BF),
            vmem((CHUNKS, HD, QW), BF),
            vmem((CHUNKS, SLOTS, width, LANES), BF),
            vmem((CHUNKS * SLOTS * LANES, 128), jnp.int32),
            vmem((1, CHUNKS * QW), F32),
            vmem((1, CHUNKS * QW), F32),
            vmem((HD, CHUNKS * QW), F32),
            vmem((CHUNKS, 2, TILE_DEV, T, 128), BF),
            vmem((HEADS, CHUNKS, T, 128), BF),
            dma((2,)), dma((7,)), dma,
            dma((CHUNKS, 8)), dma((CHUNKS, 8)),
            dma((CHUNKS, 16)), dma((CHUNKS, 16)),
            dma((CHUNKS,)), dma((CHUNKS,)),
            dma((16,)), dma((16,)),
            dma((16,)), dma((16,)),
        ],
        compiler_params=pltpu.CompilerParams(
            vmem_limit_bytes=VMEM_LIMIT, collective_id=0, has_side_effects=True
        ),
        name="slide_step",
    )(
        slide_tiles, tiles, w_reduce, w_spatial.reshape(3, 3 * MID, MID), w_expand, w_embed,
        w_query.T, w_key.T, w_value.T, w_out,
    )


def solution(mesh):
    placed = (
        P(("blk", "tile"), None, None, None),
        P(),
        P(),
        P(),
        P(),
        P(None, "tile"),
        P(None, "tile"),
        P(None, "tile"),
        P("tile", None),
        P(),
    )
    return jax.shard_map(
        shards, mesh=mesh, in_specs=placed, out_specs=P(("blk", "tile"), None), check_vma=False
    )
```

```python
import math

import jax
import jax.numpy as jnp
from jax import lax
from jax.experimental import pallas as pl
from jax.experimental.pallas import tpu as pltpu
from jax.sharding import PartitionSpec as P

C = 2048
MID = 512
HD = 96
E = 1536
HEADS = 16
TILE_DEV = 8
PER_DEV = 48
T = 16
CHUNKS = PER_DEV // T
R = T * 64
LANES = T * TILE_DEV
SHARD = PER_DEV * TILE_DEV
SLOTS = 16
QW = 2 * LANES
NEG = -1e30
RATE = 1.4426950408889634 / math.sqrt(HD)
VMEM_LIMIT = 61 << 20
MESH = pl.DeviceIdType.MESH
BF = jnp.bfloat16
F32 = jnp.float32


def normalize(rows):
    values = rows.astype(F32)
    center = jnp.mean(values, axis=1, keepdims=True)
    spread = jnp.mean((values - center) ** 2, axis=1, keepdims=True)
    return ((values - center) * lax.rsqrt(spread + 1e-05)).astype(BF)


def nt(a, b):
    return lax.dot_general(a, b, (((1,), (1,)), ((), ())), preferred_element_type=F32)


def body(
    slides, tiles, wr_hbm, ws_hbm, wx_hbm, we_hbm, wq_hbm, wk_hbm, wv_hbm, wo_hbm, o_ref,
    x_buf, wr, ws, wx, we, wqkv, wo, near, pool, emb, emb_all, q_st, kv_st, q_all, kv_all,
    key_slide, top, total, acc, att_st, att_in,
    x_sem, w_sem, own_sem, emb_send, emb_recv, kv_send, kv_recv, q_send, q_recv, att_send, att_recv,
    wo_send, wo_recv,
):
    t = lax.axis_index("tile")
    b = lax.axis_index("blk")
    core = b % 2
    half = (b // 2) % 2
    y = b // 4
    partner = b + 2 - 4 * half
    sibling = b + 1 - 2 * core
    x = t % 4
    z_lo = t // 4
    mine = 2 * y + half

    def remote(src, dst, send, recv, tile, blk):
        return pltpu.make_async_remote_copy(
            src_ref=src, dst_ref=dst, send_sem=send, recv_sem=recv,
            device_id={"tile": tile, "blk": blk}, device_id_type=MESH,
        )

    def load_x(c):
        return pltpu.make_async_copy(tiles.at[pl.ds(c * T, T)], x_buf.at[c % 2], x_sem.at[c % 2])

    weights = [
        pltpu.make_async_copy(a, v, w_sem.at[i])
        for i, (a, v) in enumerate(
            zip((wr_hbm, ws_hbm, wx_hbm, we_hbm, wk_hbm, wv_hbm, wq_hbm), (wr, ws, wx, we, wqkv.at[0], wqkv.at[1], wqkv.at[2]))
        )
    ]
    load_x(0).start()
    for copy in weights:
        copy.start()

    own_rows = pltpu.make_async_copy(wo_hbm.at[pl.ds(core * HD, HD)], wo.at[core, t], own_sem)

    def out_x(d):
        rows = wo_hbm.at[pl.ds(core * HD, HD)]
        return remote(rows, wo.at[core, t], wo_send.at[d], wo_recv.at[x], z_lo * 4 + (x + d) % 4, b)

    def from_x(d):
        src = (x + d) % 4
        there = wo.at[core, z_lo * 4 + src]
        return remote(there, there, wo_send.at[0], wo_recv.at[src], z_lo * 4 + src, b)

    def over_x(i):
        src = z_lo * 4 + (x + (1 if i else 3)) % 4
        rows = wo.at[core, src, pl.ds(48 * i, 48)]
        return remote(
            rows, rows, wo_send.at[7 + i], wo_recv.at[7 + i], z_lo * 4 + (x + (3 if i else 1)) % 4, b
        )

    def from_over_x(i):
        rows = wo.at[core, z_lo * 4 + (x + 2) % 4, pl.ds(48 * i, 48)]
        return remote(
            rows, rows, wo_send.at[0], wo_recv.at[7 + i], z_lo * 4 + (x + (1 if i else 3)) % 4, b
        )

    z = 2 * half + z_lo

    def out_z(i):
        to = (z + (3 if i else 1)) % 4
        rows = wo.at[core, pl.ds(z_lo * 4 + 2 * i, 2)]
        return remote(
            rows, rows, wo_send.at[4 + i], wo_recv.at[4 + i],
            (to % 2) * 4 + x, y * 4 + (to // 2) * 2 + core,
        )

    def from_z(i):
        src = (z + (1 if i else 3)) % 4
        rows = wo.at[core, pl.ds((1 - z_lo) * 4 + 2 * i, 2)]
        return remote(
            rows, rows, wo_send.at[0], wo_recv.at[4 + i],
            (src % 2) * 4 + x, y * 4 + (src // 2) * 2 + core,
        )

    def out_core():
        return remote(wo.at[core], wo.at[core], wo_send.at[6], wo_recv.at[6], t, sibling)

    def from_core():
        return remote(wo.at[1 - core], wo.at[1 - core], wo_send.at[6], wo_recv.at[6], t, sibling)

    def out_emb(c, d):
        return remote(
            emb.at[c], emb_all.at[c, t], emb_send.at[c, d], emb_recv.at[c, t], (t + d) % TILE_DEV, b
        )

    def from_emb(c, d):
        src = (t + d) % TILE_DEV
        return remote(emb.at[c], emb_all.at[c, src], emb_send.at[c, d], emb_recv.at[c, src], src, b)

    def slot_of(c, s):
        return kv_all.at[c, s]

    def out_kv(c, i, same):
        to = ((y + i) % 4) * 4 + core + 2 * (half if same else 1 - half)
        return remote(
            kv_st.at[c, half if same else 1 - half], slot_of(c, mine),
            kv_send.at[c, 2 * i + (0 if same else 1)], kv_recv.at[c, mine], t, to,
        )

    def from_kv(c, d):
        u = (mine + d) % 8
        return remote(
            kv_st.at[c, 0], slot_of(c, u), kv_send.at[c, 0], kv_recv.at[c, u], t, 2 * u + core
        )

    def pass_on(c):
        return remote(
            kv_all.at[c, 0:8], kv_all.at[c, 8:16], kv_send.at[c, 8], kv_recv.at[c, 8], t, sibling
        )

    def swap_q(c):
        return remote(
            q_st.at[c], q_all.at[c, :, LANES:QW], q_send.at[c], q_recv.at[c], t, partner
        )

    barrier = pltpu.get_barrier_semaphore()
    for d in range(1, TILE_DEV):
        for blk in (b, partner):
            pl.semaphore_signal(
                barrier, inc=1, device_id={"tile": (t + d) % TILE_DEV, "blk": blk}, device_id_type=MESH
            )
    for d in range(1, 8):
        pl.semaphore_signal(
            barrier, inc=1, device_id={"tile": t, "blk": 2 * ((mine + d) % 8) + core}, device_id_type=MESH
        )
    pl.semaphore_signal(barrier, inc=1, device_id={"tile": t, "blk": sibling}, device_id_type=MESH)

    near[:, 0] = jnp.zeros((T, 8, 3 * MID), BF)
    near[:, 9] = jnp.zeros((T, 8, 3 * MID), BF)
    own_rows.start()


    ends = [slides[0], slides[0] + slides[1], slides[0] + slides[1] + slides[2]]

    def slide_at(pos):
        return sum((pos >= end).astype(jnp.int32) for end in ends)

    def table(i, carry):
        n = lax.broadcasted_iota(jnp.int32, (512, 128), 0) + 512 * (i % 4)
        slot = n >> 7
        blk = 2 * (slot & 7) + jnp.where(slot < 8, core, 1 - core)
        pos = blk * SHARD + ((n >> 4) & 7) * PER_DEV + (i // 4) * T + (n & 15)
        key_slide[pl.ds(pl.multiple_of(i * 512, 512), 512), :] = slide_at(pos)
        return carry

    n = lax.broadcasted_iota(jnp.int32, (8, CHUNKS * QW), 1)
    query_pos = (
        jnp.where(((n >> 7) & 1) == 0, b, partner) * SHARD + ((n >> 4) & 7) * PER_DEV + (n >> 8) * T + (n & 15)
    )
    query_slide = slide_at(query_pos)[0:1]
    top[...] = jnp.full((1, CHUNKS * QW), NEG, F32)
    total[...] = jnp.zeros((1, CHUNKS * QW), F32)
    acc[...] = jnp.zeros((HD, CHUNKS * QW), F32)

    lax.fori_loop(0, 12, table, 0)

    def project(c):
        for d in range(1, TILE_DEV):
            from_emb(c, d).wait_recv()
        normed = normalize(emb_all[c].reshape(LANES, E))
        joined = nt(wqkv[...].reshape(6 * HD, E), normed).astype(BF)
        for h in range(2):
            kv_st[c, h, 0:HD] = joined[h * HD : (h + 1) * HD]
            kv_st[c, h, HD : 2 * HD] = joined[(2 + h) * HD : (3 + h) * HD]
        for i in range(4):
            out_kv(c, i, False).start()
            if i:
                out_kv(c, i, True).start()
        kv_all[c, mine] = kv_st[c, half]
        first, second = joined[4 * HD : 5 * HD], joined[5 * HD : 6 * HD]
        q_all[c, :, 0:LANES] = jnp.where(half == 0, first, second)
        q_st[c] = jnp.where(half == 0, second, first)
        swap_q(c).start()

    def relay(c):
        for d in range(1, 8):
            from_kv(c, d).wait_recv()
        pass_on(c).start()

    def attend(c, group, first, last):
        lanes = slice(first * QW, last * QW)
        key = jnp.concatenate([kv_all[c, group * 8 + k, 0:HD] for k in range(8)], axis=1).T
        value = jnp.concatenate([kv_all[c, group * 8 + k, HD : 2 * HD] for k in range(8)], axis=1)
        query = jnp.concatenate([q_all[i] for i in range(first, last)], axis=1)
        scores = jnp.dot(key, query, preferred_element_type=F32) * RATE
        slide = key_slide[pl.ds(pl.multiple_of(c * 2048 + group * 1024, 1024), 1024), :]
        slide = jnp.concatenate([slide] * ((last - first) * 2), axis=1)
        scores = jnp.where(slide == query_slide[:, lanes], scores, NEG)
        old = top[:, lanes]
        new = jnp.maximum(old, jnp.max(scores, axis=0, keepdims=True))
        weights = jnp.exp2(scores - new)
        keep = jnp.exp2(old - new)
        top[:, lanes] = new
        total[:, lanes] = total[:, lanes] * keep + jnp.sum(weights, axis=0, keepdims=True)
        acc[:, lanes] = acc[:, lanes] * keep + jnp.dot(
            value, weights.astype(BF), preferred_element_type=F32
        )

    def encode(c, carry):
        load_x(c).wait()

        @pl.when(c < CHUNKS - 1)
        def _():
            load_x(c + 1).start()

        def first_use(i):
            @pl.when(c == 0)
            def _():
                weights[i].wait()

        first_use(0)
        x_ref = x_buf.at[c % 2]
        r = jnp.maximum(jnp.dot(x_ref[...].reshape(R, C), wr[...], preferred_element_type=F32), 0.0)
        j = lax.broadcasted_iota(jnp.int32, (R, MID), 0) % 8
        left = jnp.where(j == 0, 0.0, pltpu.roll(r, 1, 0))
        right = jnp.where(j == 7, 0.0, pltpu.roll(r, R - 1, 0))
        for at, shifted in enumerate((left, r, right)):
            near[:, 1:9, :, at * MID : (at + 1) * MID] = shifted.astype(BF).reshape(T, 8, 8, MID)

        @pl.when(c == 0)
        def _():
            pl.semaphore_wait(barrier, 2 * (TILE_DEV - 1) + 8)
            for d in (1, 3):
                out_x(d).start()

        first_use(1)
        conv = sum(
            jnp.dot(near[:, k : k + 8].reshape(R, 3 * MID), ws[k], preferred_element_type=F32) for k in range(3)
        )
        s = jnp.maximum(conv, 0.0).astype(BF)
        first_use(2)

        @pl.when(c > 0)
        def _():
            project(c - 1)

        @pl.when(c == 1)
        def _():
            for i in range(2):
                from_over_x(i).wait_recv()
            for i in range(2):
                out_z(i).start()

        for k in range(4):
            cols = slice(k * 512, (k + 1) * 512)
            out = jnp.dot(s, wx[:, cols], preferred_element_type=F32)
            out = jnp.maximum(out + x_ref[:, :, :, cols].reshape(R, 512).astype(F32), 0.0)
            pool[:, cols] = (jnp.sum(jnp.sum(out.reshape(T, 8, 8, 512), axis=1), axis=1) * (1.0 / 64)).astype(BF)
        first_use(3)
        emb[c] = jnp.dot(pool[...], we[...], preferred_element_type=F32).astype(BF)
        for d in range(1, TILE_DEV):
            out_emb(c, d).start()
        emb_all[c, t] = emb[c]

        @pl.when(c == 0)
        def _():
            for i in range(4, 7):
                weights[i].wait()
            own_rows.wait()
            for d in (1, 3):
                from_x(d).wait_recv()
            for i in range(2):
                over_x(i).start()

        @pl.when(c > 0)
        def _():
            relay(c - 1)

        return carry

    lax.fori_loop(0, CHUNKS, encode, 0)

    def sweep(c, first, last, start=0, stop=2):
        def block(g, carry):
            attend(c, g, first, last)
            return carry

        lax.fori_loop(start, stop, block, 0)

    for c in range(2):
        swap_q(c).wait_recv()
    for c in range(2):
        pass_on(c).wait_recv()
        sweep(c, 0, 2)
    project(2)
    swap_q(2).wait_recv()
    sweep(0, 2, 3)
    relay(2)
    sweep(1, 2, 3)
    for i in range(2):
        from_z(i).wait_recv()
    out_core().start()
    attend(2, 0, 0, 3)
    pass_on(2).wait_recv()
    attend(2, 1, 0, 3)

    result = (acc[...] / total[...]).T.astype(BF)
    att_st[...] = jnp.concatenate(
        [result, jnp.zeros((CHUNKS * QW, 128 - HD), BF)], axis=1
    ).reshape(CHUNKS, 2, TILE_DEV, T, 128)
    head = 2 * t + half

    def out_att(d, s):
        to = (t + d) % TILE_DEV
        return remote(
            att_st.at[:, s, to], att_in.at[head], att_send.at[2 * d + s], att_recv.at[head], to,
            partner if s else b,
        )

    def from_att(d, s):
        src = (t + d) % TILE_DEV
        other = 2 * src + (1 - half if s else half)
        return remote(
            att_st.at[:, s, 0], att_in.at[other], att_send.at[0], att_recv.at[other], src, partner if s else b
        )

    pairs = [(d, s) for d in range(TILE_DEV) for s in range(2) if d + s]
    for d, s in pairs:
        out_att(d, s).start()
    att_in[head] = att_st[:, 0, t]
    for d in (1, 3):
        out_x(d).wait_send()
    for i in range(2):
        over_x(i).wait_send()
        out_z(i).wait_send()
    for c in range(CHUNKS):
        for d in range(1, TILE_DEV):
            out_emb(c, d).wait_send()
        for i in range(4):
            out_kv(c, i, False).wait_send()
            if i:
                out_kv(c, i, True).wait_send()
        pass_on(c).wait_send()
        swap_q(c).wait_send()
    out_core().wait_send()
    from_core().wait_recv()
    for d, s in pairs:
        from_att(d, s).wait_recv()
    attended = jnp.concatenate([att_in[2 * k + p].reshape(PER_DEV, 128)[:, 0:HD] for p in range(2) for k in range(TILE_DEV)], axis=1)
    mixed = jnp.dot(attended, wo[...].reshape(E, E), preferred_element_type=F32)
    o_ref[...] = (emb[...].reshape(PER_DEV, E).astype(F32) + mixed).astype(BF)

    for d, s in pairs:
        out_att(d, s).wait_send()


def shards(
    tiles, w_reduce, w_spatial, w_expand, w_embed, w_query, w_key, w_value, w_out, slide_tiles
):
    anywhere = pl.BlockSpec(memory_space=pl.ANY)
    dma = pltpu.SemaphoreType.DMA
    vmem = pltpu.VMEM
    width = 2 * HD
    return pl.pallas_call(
        body,
        in_specs=[pl.BlockSpec(memory_space=pltpu.SMEM)] + [anywhere] * 9,
        out_specs=pl.BlockSpec(memory_space=vmem),
        out_shape=jax.ShapeDtypeStruct((PER_DEV, E), BF),
        scratch_shapes=[
            vmem((2, T, 8, 8, C), BF),
            vmem((C, MID), BF),
            vmem((3, 3 * MID, MID), BF),
            vmem((MID, C), BF),
            vmem((C, E), BF),
            vmem((3, width, E), BF),
            vmem((2, TILE_DEV, HD, E), BF),
            vmem((T, 10, 8, 3 * MID), BF),
            vmem((T, C), BF),
            vmem((CHUNKS, T, E), BF),
            vmem((CHUNKS, TILE_DEV, T, E), BF),
            vmem((CHUNKS, HD, LANES), BF),
            vmem((CHUNKS, 2, width, LANES), BF),
            vmem((CHUNKS, HD, QW), BF),
            vmem((CHUNKS, SLOTS, width, LANES), BF),
            vmem((CHUNKS * SLOTS * LANES, 128), jnp.int32),
            vmem((1, CHUNKS * QW), F32),
            vmem((1, CHUNKS * QW), F32),
            vmem((HD, CHUNKS * QW), F32),
            vmem((CHUNKS, 2, TILE_DEV, T, 128), BF),
            vmem((HEADS, CHUNKS, T, 128), BF),
            dma((2,)), dma((7,)), dma,
            dma((CHUNKS, 8)), dma((CHUNKS, 8)),
            dma((CHUNKS, 16)), dma((CHUNKS, 16)),
            dma((CHUNKS,)), dma((CHUNKS,)),
            dma((16,)), dma((16,)),
            dma((16,)), dma((16,)),
        ],
        compiler_params=pltpu.CompilerParams(
            vmem_limit_bytes=VMEM_LIMIT, collective_id=0, has_side_effects=True
        ),
        name="slide_step",
    )(
        slide_tiles, tiles, w_reduce, w_spatial.reshape(3, 3 * MID, MID), w_expand, w_embed,
        w_query.T, w_key.T, w_value.T, w_out,
    )


def solution(mesh):
    placed = (
        P(("blk", "tile"), None, None, None),
        P(),
        P(),
        P(),
        P(),
        P(None, "tile"),
        P(None, "tile"),
        P(None, "tile"),
        P("tile", None),
        P(),
    )
    return jax.shard_map(
        shards, mesh=mesh, in_specs=placed, out_specs=P(("blk", "tile"), None), check_vma=False
    )
```
